32 devices in a mesh: grp: 2 (over x), tm: 16 (over z, y, core).
Axes of the slice: x: 2, y: 2, z: 4, core: 2. Of those that a mesh axis runs over, the one named last changes fastest.
Arguments:
- features: bfloat16 [128, 16, 4608], P(('grp', 'tm')), parts along dimension 0, may hold values from -6 to 6
- gains: float32 [4, 192], replicated, may hold values from 0.1 to 1.9
- conv_weights: bfloat16 [4, 3, 3, 3, 192, 192], replicated, may hold values from -0.078125 to 0.078125
- video_frames: int32 [8], P('grp'), parts along dimension 0, may hold values from 1 to 48, as said below
- video_start: int32 [8], P('grp'), parts along dimension 0, may hold values from 0 to 15, as said below
Outputs:
- decoded: bfloat16 [128, 16, 4608], P(('grp', 'tm')), parts along dimension 0
The draws below stay inside these ranges and needn't reach their ends.
There are 2 independent parts, one for each index of `grp`. The reference program is written for one: setup_inputs(seed, part) draws one part's arguments, and reference() takes and returns one part's arrays. A program takes and returns all parts, laid end to end along the dimension named above; an argument that names none is the same for every part. Nothing has to cross between parts.
Inputs may be any that keep to these rules, and one draw needn't show every extreme that they name: video_start[0] = 0 and the starts rise strictly; video v takes the spans from video_start[v] up to the next video's start (16 for the last), and the videos fill all spans. `video_frames`: video v has its number of spans times 4 frames, less 0 to 3 empty slots at the end of its last span; the last video has 2 spans and 3 empty slots; one other video has 12 spans and no empty slot; the rest have one span each.
All inputs are finite; a program needn't handle non-finite values.
Results may differ from the reference program's by a relative error of at most 0.0056.
Values may be sent and summed in bfloat16 or wider, within the bound.
No kernel may reach another device: no remote copies, remote signals or barrier semaphores. Data moves between devices by JAX's collectives and lax.ppermute only.
A program may use at most 64 MiB of HBM per device.

```python
import jax
import jax.numpy as jnp
from jax import lax

CH = 192
FRAMES = 4
ROWS = 16
COLS = 24
VIDS = 4
TFRAMES = 64
N_TM = 16


def video_layout(key):
    layout_key = jax.random.fold_in(key, 17)
    long_key, slack_key = jax.random.split(layout_key)
    long_video = jax.random.randint(long_key, (), 0, VIDS - 1).astype(jnp.int32)
    video_ids = jnp.arange(VIDS, dtype=jnp.int32)
    is_long = video_ids == long_video
    is_final = video_ids == VIDS - 1
    span_counts = jnp.where(is_long, N_TM - VIDS, 1).astype(jnp.int32)
    span_counts = jnp.where(is_final, 2, span_counts).astype(jnp.int32)
    starts = jnp.concatenate([jnp.zeros((1,), jnp.int32), jnp.cumsum(span_counts)[:-1].astype(jnp.int32)])
    slack = jax.random.randint(slack_key, (VIDS,), 0, FRAMES).astype(jnp.int32)
    slack = jnp.where(is_long, 0, slack).astype(jnp.int32)
    slack = jnp.where(is_final, FRAMES - 1, slack).astype(jnp.int32)
    frame_counts = span_counts * FRAMES - slack
    return (starts, frame_counts)


def draw_video_frames(key, part):
    starts, frame_counts = video_layout(key)
    return frame_counts


def draw_video_start(key, part):
    starts, frame_counts = video_layout(key)
    return starts


def steps_of(rng, shape, cuts, smallest, high):
    gain, own = 1.0, jax.random.fold_in(rng, 6)
    for dim, parts in cuts:
        steps = jnp.exp(jax.random.uniform(jax.random.fold_in(own, dim), (parts,), jnp.float32, smallest / len(cuts), high / len(cuts)))
        gain = gain * jnp.repeat(steps, shape[dim] // parts).reshape([-1 if axis == dim else 1 for axis in range(len(shape))])
    return gain


def bell_draw(stream_key, shape, width, bound, cuts=(), kind=jnp.bfloat16):
    factor_of = steps_of(stream_key, shape, cuts, -0.22, 0.18) if cuts else 1.0
    values = jax.random.normal(stream_key, shape, jnp.float32) * width * factor_of
    return jnp.minimum(jnp.maximum(values, -bound), bound).astype(kind)


def setup_inputs(seed: int = 0, part: int = 0) -> dict:
    key_of = jax.random.split(jax.random.key(seed), 6)
    own_keys = jax.random.split(jax.random.fold_in(key_of[5], part), 6)
    features = bell_draw(own_keys[0], (TFRAMES, ROWS, COLS * CH), 1.0, 6.0, ((0, 16),))
    gains = jnp.clip(1.0 + 0.18 * jax.random.normal(key_of[1], (4, CH), jnp.float32), 0.1, 1.9)
    conv_weights = bell_draw(key_of[2], (4, 3, 3, 3, CH, CH), (27 * CH) ** -0.5, 0.078125)
    video_frames = draw_video_frames(jax.random.fold_in(jax.random.fold_in(key_of[5], part), 71), part)
    video_start = draw_video_start(jax.random.fold_in(jax.random.fold_in(key_of[5], part), 71), part)
    return dict(features=features, gains=gains, conv_weights=conv_weights, video_frames=video_frames, video_start=video_start)


def normalize_act(values, gain_row):
    widened = values.astype(jnp.float32)
    scaled = widened * lax.rsqrt(lax.optimization_barrier(jnp.mean(widened * widened, axis=-1, keepdims=True)) + 1e-06) * gain_row
    return jax.nn.silu(scaled).astype(jnp.bfloat16)

def causal_conv(operand, weight, video_id):
    summed = jnp.zeros(operand.shape[:3] + (weight.shape[-1],), jnp.float32)
    for tap_index in range(3):
        frame_lag = 2 - tap_index
        if frame_lag == 0:
            source = operand
        else:
            padding = jnp.zeros((frame_lag,) + operand.shape[1:], operand.dtype)
            source = jnp.concatenate([padding, operand[:-frame_lag]], axis=0)
            earlier = jnp.concatenate([jnp.full((frame_lag,), -1, jnp.int32), video_id[:-frame_lag]], axis=0)
            same_video = earlier == video_id
            source = jnp.where(same_video[:, None, None, None], source, jnp.zeros_like(source))
        summed = summed + lax.conv_general_dilated(source.astype(jnp.float32), weight[tap_index].astype(jnp.float32), (1, 1), ((1, 1), (1, 1)), dimension_numbers=('NHWC', 'HWIO', 'NHWC'), precision=lax.Precision.HIGHEST)
    return summed

def reference(features, gains, conv_weights, video_frames, video_start):
    total_frames = features.shape[0]
    frame_index = jnp.arange(total_frames, dtype=jnp.int32)
    span_index = frame_index // FRAMES
    video_id = lax.optimization_barrier(jnp.sum((span_index[:, None] >= video_start[None, :]).astype(jnp.int32), axis=1)) - 1
    position = frame_index - video_start[video_id] * FRAMES
    live_mask = position < video_frames[video_id]
    current = features.reshape(total_frames, ROWS, COLS, CH)
    for layer_pair in range(2):
        normed_in = normalize_act(current, gains[2 * layer_pair])
        hidden = causal_conv(normed_in, conv_weights[2 * layer_pair], video_id)
        normed_mid = normalize_act(hidden, gains[2 * layer_pair + 1])
        branch = causal_conv(normed_mid, conv_weights[2 * layer_pair + 1], video_id)
        current = (current.astype(jnp.float32) + branch).astype(jnp.bfloat16)
    result = jnp.where(live_mask[:, None, None, None], current, jnp.zeros_like(current))
    return result.reshape(total_frames, ROWS, COLS * CH)
```

```python
import functools

import jax
import jax.numpy as jnp
from jax import lax
from jax.experimental import pallas as pl
from jax.experimental.pallas import tpu as pltpu
from jax.sharding import PartitionSpec as P

LANES = 128
HALO = 2
STEP = 4
VMEM = pltpu.VMEM


def passed_along(value, axis):
    count = lax.axis_size(axis)
    return lax.ppermute(value, axis, [(i, i + 1) for i in range(count - 1)])


def low_half(shape):
    return lax.broadcasted_iota(jnp.int32, shape, len(shape) - 1) < LANES // 2


def swap_half(value):
    return pltpu.roll(value, LANES // 2, axis=value.ndim - 1)


def activate(main, rest, gain_main, gain_rest, channels):
    total = jnp.sum(main * main + rest * rest, axis=-1, keepdims=True)
    inverse = lax.rsqrt(total * (1.0 / channels) + 1e-06)

    def silu(value, gain):
        scaled = value * inverse * gain
        half = 0.5 * scaled
        return half * jnp.tanh(half) + half

    return silu(main, gain_main), silu(rest, gain_rest)


def load_gain(gains, gain_pad, index):
    return gain_pad[index, 0][None, None, :], gain_pad[index, 1][None, None, :]


def fill_gain(gains, gain_pad):
    count, channels = gains.shape
    gain_pad[...] = jnp.zeros_like(gain_pad)
    for k in range(count):
        gain_pad[k, 0:1, :] = gains[k : k + 1, 0:LANES]
        gain_pad[k, 1:2, 0 : channels - LANES] = gains[k : k + 1, LANES:channels]


def unpack_dense(source, frame, chunk):
    rows = source.shape[1]
    width = STEP * 192
    block = source[frame, :, pl.ds(pl.multiple_of(chunk * width, LANES), width)].astype(jnp.float32)
    tile = [block[:, LANES * i : LANES * (i + 1)] for i in range(width // LANES)]
    low = low_half((rows, LANES))
    main, rest = [], []
    for i in range(0, len(tile), 3):
        rolled_b, rolled_c = swap_half(tile[i + 1]), swap_half(tile[i + 2])
        main += [tile[i], jnp.where(low, rolled_b, rolled_c)]
        rest += [jnp.where(low, tile[i + 1], 0.0), jnp.where(low, rolled_c, 0.0)]
    return jnp.stack(main), jnp.stack(rest)


def pack_dense(target, frame, chunk, main, rest):
    rows = target.shape[1]
    width = STEP * 192
    low = low_half((rows, LANES))
    tile = []
    for i in range(0, STEP, 2):
        rolled = swap_half(main[i + 1])
        tile += [main[i], jnp.where(low, rest[i], rolled), jnp.where(low, rolled, swap_half(rest[i + 1]))]
    block = jnp.concatenate(tile, axis=-1).astype(target.dtype)
    target[frame, :, pl.ds(pl.multiple_of(chunk * width, LANES), width)] = block


def unpack_wire(source, frame, chunk, keep):
    cols = source.shape[1] * 2 // 3
    main = source[frame, pl.ds(STEP * chunk, STEP)].astype(jnp.float32)
    pair = source[frame, pl.ds(cols + STEP // 2 * chunk, STEP // 2)].astype(jnp.float32)
    low = low_half(pair.shape)
    rest = jnp.stack([jnp.where(low, pair, 0.0), jnp.where(low, swap_half(pair), 0.0)], axis=1)
    return main * keep, rest.reshape(main.shape) * keep


def pack_wire(target, frame, chunk, main, rest):
    cols = target.shape[1] * 2 // 3
    target[frame, pl.ds(STEP * chunk, STEP)] = main.astype(target.dtype)
    pair = rest.reshape((STEP // 2, 2) + rest.shape[1:])
    target[frame, pl.ds(cols + STEP // 2 * chunk, STEP // 2)] = (pair[:, 0] + swap_half(pair[:, 1])).astype(target.dtype)


def clear_borders(buf):
    frames, slots, rows, lanes = buf.shape
    for frame in range(frames):
        for slot in (0, slots - 2, slots - 1):
            buf[frame, slot] = jnp.zeros((rows, lanes), buf.dtype)


def store_pieces(buf, frame, chunk, main, rest):
    rows = main.shape[1]
    row = lax.broadcasted_iota(jnp.int32, main.shape, 1)

    def above(value):
        return jnp.where(row == 0, 0.0, pltpu.roll(value, 1, axis=1))

    def below(value):
        return jnp.where(row == rows - 1, 0.0, pltpu.roll(value, rows - 1, axis=1))

    def put(first_slot, lane, value):
        buf[frame, pl.ds(first_slot, STEP), :, lane : lane + value.shape[-1]] = value.astype(buf.dtype)

    slot = STEP * chunk + 1
    put(slot, 0, above(main))
    put(slot, LANES, main)
    put(slot, 2 * LANES, below(main))
    put(slot, 3 * LANES, above(rest) + swap_half(rest))
    lower = below(rest)
    put(slot, 4 * LANES, lower[..., : LANES // 2])
    put(slot - 1, 4 * LANES + LANES // 2, lower[..., : LANES // 2])


def convolve(buf, frame, weight, layer, hidden):
    rows = buf.shape[2]
    cols = buf.shape[1] - 2
    channels = weight.shape[-1]
    span = channels - LANES

    def piece(tap, col, lane):
        return buf[frame + tap, col : col + cols, :, lane : lane + LANES].reshape(cols * rows, LANES)

    def taken(tap, row, col, rest):
        index = (tap * 3 + row) * 3 + col
        return weight[layer, index, LANES:channels, :] if rest else weight[layer, index, 0:LANES, :]

    total = None
    for tap in range(3):
        lhs, rhs = [], []
        for col in range(3):
            for row in range(3):
                lhs.append(piece(tap, col, LANES * row))
                rhs.append(taken(tap, row, col, False))
            lhs.append(piece(tap, col, 3 * LANES))
            rhs += [taken(tap, 0, col, True), taken(tap, 1, col, True)]
        lhs.append(piece(tap, 0, 4 * LANES))
        rhs += [taken(tap, 2, 0, True), taken(tap, 2, 1, True)]
        lhs.append(piece(tap, 2, 4 * LANES))
        rhs += [taken(tap, 2, 2, True), jnp.zeros((span, channels), weight.dtype)]
        part = jnp.dot(
            jnp.concatenate(lhs, axis=1), jnp.concatenate(rhs, axis=0), preferred_element_type=jnp.float32
        )
        total = part if total is None else total + part
    hidden[0] = total[:, :LANES].reshape(cols, rows, LANES)
    hidden[1, :, :, 0:span] = total[:, LANES:].reshape(cols, rows, span)


def each_chunk(cols, body):
    lax.fori_loop(0, cols // STEP, lambda i, carry: (body(i), carry)[1], 0)


def each_frame(count, body):
    lax.fori_loop(0, count, lambda i, carry: (body(i), carry)[1], 0)


def hidden_chunk(hidden, chunk):
    return hidden[0, pl.ds(STEP * chunk, STEP)], hidden[1, pl.ds(STEP * chunk, STEP)]


def own_span(starts, frames):
    span = lax.axis_index("tm")
    own_start, own_frames = starts[0], frames[0]
    for v in range(1, starts.shape[0]):
        here = starts[v] <= span
        own_start = jnp.where(here, starts[v], own_start)
        own_frames = jnp.where(here, frames[v], own_frames)
    return span, own_start, own_frames


def keep_factor(starts, frames):
    span, own_start, _ = own_span(starts, frames)
    return jnp.where(span - 1 >= own_start, 1.0, 0.0).astype(jnp.float32)


def first_kernel(dense, gains, weight_hbm, first, second, wire, weight, hidden, gain_pad, sem):
    copy = pltpu.make_async_copy(weight_hbm.at[pl.ds(0, 1)], weight, sem)
    copy.start()
    cols = first.shape[1] - 2
    channels = gains.shape[1]
    fill_gain(gains, gain_pad)
    clear_borders(first)
    clear_borders(second)
    hidden[1] = jnp.zeros_like(hidden[1])

    def enter(frame):
        def body(chunk):
            main, rest = unpack_dense(dense, frame, chunk)
            main, rest = activate(main, rest, *load_gain(gains, gain_pad, 0), channels)
            store_pieces(first, frame + HALO, chunk, main, rest)

        each_chunk(cols, body)

    each_frame(dense.shape[0], enter)
    copy.wait()
    hidden_out(first, HALO, weight, 0, hidden, gains, gain_pad, 1, second, wire)


def hidden_out(source, base, weight, layer, hidden, gains, gain_pad, gain_index, target, wire):
    cols = source.shape[1] - 2
    channels = gains.shape[1]

    def frame_body(i):
        convolve(source, base + i, weight, layer, hidden)

        def body(chunk):
            main, rest = activate(*hidden_chunk(hidden, chunk), *load_gain(gains, gain_pad, gain_index), channels)
            store_pieces(target, base + HALO + i, chunk, main, rest)
            if wire is not None:
                pack_wire(wire, i, chunk, main, rest)

        each_chunk(cols, body)

    each_frame(HALO, frame_body)


def residual_out(source, base, weight, layer, hidden, finish):
    cols = source.shape[1] - 2

    def frame_body(i):
        convolve(source, base + i, weight, layer, hidden)
        each_chunk(cols, lambda chunk: finish(i, chunk, *hidden_chunk(hidden, chunk)))

    each_frame(HALO, frame_body)


def rounded(value):
    return value.astype(jnp.bfloat16).astype(jnp.float32)


def state_put(state, i, chunk, main, rest):
    state[i, 0, pl.ds(STEP * chunk, STEP)] = main.astype(state.dtype)
    state[i, 1, pl.ds(STEP * chunk, STEP)] = rest.astype(state.dtype)


def state_get(state, i, chunk):
    return (
        state[i, 0, pl.ds(STEP * chunk, STEP)].astype(jnp.float32),
        state[i, 1, pl.ds(STEP * chunk, STEP)].astype(jnp.float32),
    )


def halo_in(wire, target, keep):
    cols = target.shape[1] - 2

    def frame_body(frame):
        each_chunk(cols, lambda chunk: store_pieces(target, frame, chunk, *unpack_wire(wire, frame, chunk, keep)))

    each_frame(HALO, frame_body)


def second_kernel(
    starts, frames, dense_halo, dense, gains, weight, first_in, second_in, first, second, third, state, wire, hidden, gain_pad
):
    cols = first.shape[1] - 2
    channels = gains.shape[1]
    keep = keep_factor(starts, frames)
    fill_gain(gains, gain_pad)
    clear_borders(third)
    hidden[1] = jnp.zeros_like(hidden[1])

    def enter(frame):
        def body(chunk):
            main, rest = unpack_dense(dense_halo, frame, chunk)
            main, rest = activate(main, rest, *load_gain(gains, gain_pad, 0), channels)
            store_pieces(first, frame, chunk, main * keep, rest * keep)

        each_chunk(cols, body)

    each_frame(HALO, enter)
    hidden_out(first, 0, weight, 0, hidden, gains, gain_pad, 1, second, None)

    def finish(i, chunk, main, rest):
        main_in, rest_in = unpack_dense(dense, HALO + i, chunk)
        main, rest = rounded(main + main_in), rounded(rest + rest_in)
        state_put(state, i, chunk, main, rest)
        main, rest = activate(main, rest, *load_gain(gains, gain_pad, 2), channels)
        store_pieces(third, 2 * HALO + i, chunk, main, rest)
        pack_wire(wire, i, chunk, main, rest)

    residual_out(second, HALO, weight, 1, hidden, finish)


def third_kernel(
    starts, frames, halo, dense, gains, weight, second_in, third_in, second, third, fourth, state, wire, hidden, gain_pad
):
    channels = gains.shape[1]
    keep = keep_factor(starts, frames)
    fill_gain(gains, gain_pad)
    clear_borders(fourth)
    hidden[1] = jnp.zeros_like(hidden[1])
    halo_in(halo, second, keep)

    def finish(i, chunk, main, rest):
        main_in, rest_in = unpack_dense(dense, i, chunk)
        main, rest = rounded(main + main_in), rounded(rest + rest_in)
        state_put(state, i, chunk, main, rest)
        main, rest = activate(main, rest, *load_gain(gains, gain_pad, 2), channels)
        store_pieces(third, HALO + i, chunk, main, rest)

    residual_out(second, 0, weight, 1, hidden, finish)
    hidden_out(third, HALO, weight, 2, hidden, gains, gain_pad, 3, fourth, wire)


def live_factor(starts, frames, frame, span_frames):
    span, own_start, own_frames = own_span(starts, frames)
    return jnp.where((span - own_start) * span_frames + frame < own_frames, 1.0, 0.0).astype(jnp.float32)


def fourth_kernel(
    starts, frames, halo, gains, weight, third_in, fourth_in, state, third, fourth, out, hidden, gain_pad
):
    keep = keep_factor(starts, frames)
    fill_gain(gains, gain_pad)
    hidden[1] = jnp.zeros_like(hidden[1])
    halo_in(halo, third, keep)
    hidden_out(third, 0, weight, 2, hidden, gains, gain_pad, 3, fourth, None)

    def finish(i, chunk, main, rest):
        main_in, rest_in = state_get(state, i, chunk)
        live = live_factor(starts, frames, HALO + i, 2 * HALO)
        pack_dense(out, i, chunk, (main + main_in) * live, (rest + rest_in) * live)

    residual_out(fourth, HALO, weight, 3, hidden, finish)


def fifth_kernel(starts, frames, halo, weight, fourth_in, state, later, fourth, out, hidden):
    keep = keep_factor(starts, frames)
    hidden[1] = jnp.zeros_like(hidden[1])
    halo_in(halo, fourth, keep)
    out[HALO:] = later[...]

    def finish(i, chunk, main, rest):
        main_in, rest_in = state_get(state, i, chunk)
        live = live_factor(starts, frames, i, 2 * HALO)
        pack_dense(out, i, chunk, (main + main_in) * live, (rest + rest_in) * live)

    residual_out(fourth, 0, weight, 3, hidden, finish)


def local(features, gains, conv_weights, video_frames, video_start):
    frames, rows, merged = features.shape
    channels = gains.shape[1]
    cols = merged // channels
    layers = conv_weights.shape[0]
    weight = conv_weights.reshape(layers, 27, channels, channels)
    bf16, f32 = jnp.bfloat16, jnp.float32
    pieces = jax.ShapeDtypeStruct((frames + HALO, cols + 2, rows, 5 * LANES), bf16)
    wire = jax.ShapeDtypeStruct((HALO, cols * 3 // 2, rows, LANES), bf16)
    state = jax.ShapeDtypeStruct((HALO, 2, cols, rows, LANES), bf16)
    hidden = VMEM((2, cols, rows, LANES), f32)
    gain_pad = VMEM((layers, 2, LANES), f32)
    smem = pl.BlockSpec(memory_space=pltpu.SMEM)
    vmem = pl.BlockSpec(memory_space=VMEM)
    hbm = pl.BlockSpec(memory_space=pltpu.HBM)

    def call(body, ins, outs, scratch, convs, aliases=None, name=None):
        return pl.pallas_call(
            body,
            out_shape=outs,
            in_specs=ins,
            out_specs=tuple(vmem for _ in outs),
            scratch_shapes=scratch,
            input_output_aliases=aliases or {},
            name=name,
            compiler_params=pltpu.CompilerParams(vmem_limit_bytes=12 << 20),
            cost_estimate=pl.CostEstimate(
                flops=convs * 2 * 27 * channels * channels * rows * cols * 2,
                bytes_accessed=4 << 20,
                transcendentals=0,
            ),
        )

    halo0 = passed_along(features[frames - HALO :], "tm")
    first, second, wire1 = call(
        first_kernel,
        [vmem, vmem, hbm],
        (pieces, pieces, wire),
        [VMEM((1, 27, channels, channels), bf16), hidden, gain_pad, pltpu.SemaphoreType.DMA],
        1,
        name="k1",
    )(features, gains, weight)
    halo1 = passed_along(wire1, "tm")
    _, second, third, state_late, wire2 = call(
        second_kernel,
        [smem, smem] + [vmem] * 6,
        (pieces, pieces, pieces, state, wire),
        [hidden, gain_pad],
        2,
        {6: 0, 7: 1},
        name="k2",
    )(video_start, video_frames, halo0, features, gains, weight, first, second)
    halo2 = passed_along(wire2, "tm")
    _, third, fourth, state_early, wire3 = call(
        third_kernel,
        [smem, smem] + [vmem] * 6,
        (pieces, pieces, pieces, state, wire),
        [hidden, gain_pad],
        2,
        {6: 0, 7: 1},
        name="k3",
    )(video_start, video_frames, halo1, features, gains, weight, second, third)
    halo3 = passed_along(wire3, "tm")
    dense_half = jax.ShapeDtypeStruct((HALO, rows, merged), bf16)
    _, fourth, later = call(
        fourth_kernel,
        [smem, smem] + [vmem] * 6,
        (pieces, pieces, dense_half),
        [hidden, gain_pad],
        2,
        {5: 0, 6: 1},
        name="k4",
    )(video_start, video_frames, halo2, gains, weight, third, fourth, state_late)
    _, out = call(
        fifth_kernel,
        [smem, smem] + [vmem] * 5,
        (pieces, jax.ShapeDtypeStruct(features.shape, bf16)),
        [hidden],
        1,
        {4: 0},
        name="k5",
    )(video_start, video_frames, halo3, weight, fourth, state_early, later)
    return out


def solution(mesh):
    in_specs = (P(("grp", "tm"), None, None), P(), P(), P("grp"), P("grp"))
    out_specs = P(("grp", "tm"), None, None)
    return jax.shard_map(local, mesh=mesh, in_specs=in_specs, out_specs=out_specs, check_vma=False)
```

```python
import functools

import jax
import jax.numpy as jnp
from jax import lax
from jax.experimental import pallas as pl
from jax.experimental.pallas import tpu as pltpu
from jax.sharding import PartitionSpec as P

LANES = 128
HALO = 2
STEP = 4
VMEM = pltpu.VMEM


def passed_along(value, axis):
    count = lax.axis_size(axis)
    return lax.ppermute(value, axis, [(i, i + 1) for i in range(count - 1)])


def low_half(shape):
    return lax.broadcasted_iota(jnp.int32, shape, len(shape) - 1) < LANES // 2


def swap_half(value):
    return pltpu.roll(value, LANES // 2, axis=value.ndim - 1)


def activate(main, rest, gain_main, gain_rest, channels):
    total = jnp.sum(main * main + rest * rest, axis=-1, keepdims=True)
    inverse = lax.rsqrt(total * (1.0 / channels) + 1e-06)

    def silu(value, gain):
        scaled = value * inverse * gain
        half = 0.5 * scaled
        return half * jnp.tanh(half) + half

    return silu(main, gain_main), silu(rest, gain_rest)


def load_gain(gains, gain_pad, index):
    return gain_pad[index, 0][None, None, :], gain_pad[index, 1][None, None, :]


def fill_gain(gains, gain_pad):
    count, channels = gains.shape
    gain_pad[...] = jnp.zeros_like(gain_pad)
    for k in range(count):
        gain_pad[k, 0:1, :] = gains[k : k + 1, 0:LANES]
        gain_pad[k, 1:2, 0 : channels - LANES] = gains[k : k + 1, LANES:channels]


def unpack_dense(source, frame, chunk):
    rows = source.shape[1]
    width = STEP * 192
    block = source[frame, :, chunk * width : (chunk + 1) * width].astype(jnp.float32)
    tile = [block[:, LANES * i : LANES * (i + 1)] for i in range(width // LANES)]
    low = low_half((rows, LANES))
    main, rest = [], []
    for i in range(0, len(tile), 3):
        rolled_b, rolled_c = swap_half(tile[i + 1]), swap_half(tile[i + 2])
        main += [tile[i], jnp.where(low, rolled_b, rolled_c)]
        rest += [jnp.where(low, tile[i + 1], 0.0), jnp.where(low, rolled_c, 0.0)]
    return jnp.stack(main), jnp.stack(rest)


def pack_dense(target, frame, chunk, main, rest):
    rows = target.shape[1]
    width = STEP * 192
    low = low_half((rows, LANES))
    tile = []
    for i in range(0, STEP, 2):
        rolled = swap_half(main[i + 1])
        tile += [main[i], jnp.where(low, rest[i], rolled), jnp.where(low, rolled, swap_half(rest[i + 1]))]
    block = jnp.concatenate(tile, axis=-1).astype(target.dtype)
    target[frame, :, chunk * width : (chunk + 1) * width] = block


def unpack_wire(source, frame, chunk, keep):
    cols = source.shape[1] * 2 // 3
    main = source[frame, pl.ds(STEP * chunk, STEP)].astype(jnp.float32)
    pair = source[frame, pl.ds(cols + STEP // 2 * chunk, STEP // 2)].astype(jnp.float32)
    low = low_half(pair.shape)
    rest = jnp.stack([jnp.where(low, pair, 0.0), jnp.where(low, swap_half(pair), 0.0)], axis=1)
    return main * keep, rest.reshape(main.shape) * keep


def pack_wire(target, frame, chunk, main, rest):
    cols = target.shape[1] * 2 // 3
    target[frame, pl.ds(STEP * chunk, STEP)] = main.astype(target.dtype)
    pair = rest.reshape((STEP // 2, 2) + rest.shape[1:])
    target[frame, pl.ds(cols + STEP // 2 * chunk, STEP // 2)] = (pair[:, 0] + swap_half(pair[:, 1])).astype(target.dtype)


def clear_borders(buf):
    frames, slots, rows, lanes = buf.shape
    for frame in range(frames):
        for slot in (0, slots - 2, slots - 1):
            buf[frame, slot] = jnp.zeros((rows, lanes), buf.dtype)


def store_pieces(buf, frame, chunk, main, rest):
    rows = main.shape[1]
    row = lax.broadcasted_iota(jnp.int32, main.shape, 1)

    def above(value):
        return jnp.where(row == 0, 0.0, pltpu.roll(value, 1, axis=1))

    def below(value):
        return jnp.where(row == rows - 1, 0.0, pltpu.roll(value, rows - 1, axis=1))

    def put(first_slot, lane, value):
        buf[frame, pl.ds(first_slot, STEP), :, lane : lane + value.shape[-1]] = value.astype(buf.dtype)

    slot = STEP * chunk + 1
    put(slot, 0, above(main))
    put(slot, LANES, main)
    put(slot, 2 * LANES, below(main))
    put(slot, 3 * LANES, above(rest) + swap_half(rest))
    lower = below(rest)
    put(slot, 4 * LANES, lower[..., : LANES // 2])
    put(slot - 1, 4 * LANES + LANES // 2, lower[..., : LANES // 2])


def convolve(buf, frame, weight, layer, hidden, slot):
    rows = buf.shape[2]
    cols = buf.shape[1] - 2
    channels = weight.shape[-1]
    span = channels - LANES

    def piece(tap, col, lane):
        return buf[frame + tap, col : col + cols, :, lane : lane + LANES].reshape(cols * rows, LANES)

    def taken(tap, row, col, rest):
        index = (tap * 3 + row) * 3 + col
        return weight[layer, index, LANES:channels, :] if rest else weight[layer, index, 0:LANES, :]

    lhs, rhs = [], []
    for tap in (2, 1, 0):
        for col in range(3):
            for row in range(3):
                lhs.append(piece(tap, col, LANES * row))
                rhs.append(taken(tap, row, col, False))
            lhs.append(piece(tap, col, 3 * LANES))
            rhs += [taken(tap, 0, col, True), taken(tap, 1, col, True)]
        lhs.append(piece(tap, 0, 4 * LANES))
        rhs += [taken(tap, 2, 0, True), taken(tap, 2, 1, True)]
        lhs.append(piece(tap, 2, 4 * LANES))
        rhs += [taken(tap, 2, 2, True), jnp.zeros((span, channels), weight.dtype)]
    total = jnp.dot(jnp.concatenate(lhs, axis=1), jnp.concatenate(rhs, axis=0), preferred_element_type=jnp.float32)
    hidden[slot, 0] = total[:, :LANES].reshape(cols, rows, LANES)
    hidden[slot, 1, :, :, 0:span] = total[:, LANES:].reshape(cols, rows, span)


def each_chunk(cols, body):
    for chunk in range(cols // STEP):
        body(chunk)


def each_frame(count, body):
    for index in range(count):
        body(index)


def hidden_chunk(hidden, slot, chunk):
    return hidden[slot, 0, pl.ds(STEP * chunk, STEP)], hidden[slot, 1, pl.ds(STEP * chunk, STEP)]


def own_span(starts, frames):
    span = lax.axis_index("tm")
    own_start, own_frames = starts[0], frames[0]
    for v in range(1, starts.shape[0]):
        here = starts[v] <= span
        own_start = jnp.where(here, starts[v], own_start)
        own_frames = jnp.where(here, frames[v], own_frames)
    return span, own_start, own_frames


def keep_factor(starts, frames):
    span, own_start, _ = own_span(starts, frames)
    return jnp.where(span - 1 >= own_start, 1.0, 0.0).astype(jnp.float32)


def first_kernel(dense_hbm, gains_hbm, weight_hbm, first, second, wire, dense, gains, weight, hidden, gain_pad, sems):
    copies = [
        pltpu.make_async_copy(gains_hbm, gains, sems.at[0]),
        pltpu.make_async_copy(dense_hbm, dense, sems.at[1]),
        pltpu.make_async_copy(weight_hbm.at[pl.ds(0, 1)], weight, sems.at[2]),
    ]
    for copy in copies:
        copy.start()
    cols = first.shape[1] - 2
    channels = gains.shape[1]
    clear_borders(first)
    clear_borders(second)
    hidden[:, 1] = jnp.zeros_like(hidden[:, 1])
    copies[0].wait()
    fill_gain(gains, gain_pad)
    copies[1].wait()

    def enter(frame):
        def body(chunk):
            main, rest = unpack_dense(dense, frame, chunk)
            main, rest = activate(main, rest, *load_gain(gains, gain_pad, 0), channels)
            store_pieces(first, frame + HALO, chunk, main, rest)

        each_chunk(cols, body)

    each_frame(dense.shape[0], enter)
    copies[2].wait()
    hidden_out(first, HALO, weight, 0, hidden, gains, gain_pad, 1, second, wire)


def hidden_out(source, base, weight, layer, hidden, gains, gain_pad, gain_index, target, wire):
    cols = source.shape[1] - 2
    channels = gains.shape[1]

    def frame_body(i):
        convolve(source, base + i, weight, layer, hidden, 2 * (layer % 2) + i)

        def body(chunk):
            main, rest = activate(*hidden_chunk(hidden, 2 * (layer % 2) + i, chunk), *load_gain(gains, gain_pad, gain_index), channels)
            store_pieces(target, base + HALO + i, chunk, main, rest)
            if wire is not None:
                pack_wire(wire, i, chunk, main, rest)

        each_chunk(cols, body)

    each_frame(HALO, frame_body)


def residual_out(source, base, weight, layer, hidden, finish):
    cols = source.shape[1] - 2

    def frame_body(i):
        convolve(source, base + i, weight, layer, hidden, 2 * (layer % 2) + i)
        each_chunk(cols, lambda chunk: finish(i, chunk, *hidden_chunk(hidden, 2 * (layer % 2) + i, chunk)))

    each_frame(HALO, frame_body)


def rounded(value):
    return value.astype(jnp.bfloat16).astype(jnp.float32)


def state_put(state, i, chunk, main, rest):
    state[i, 0, pl.ds(STEP * chunk, STEP)] = main.astype(state.dtype)
    state[i, 1, pl.ds(STEP * chunk, STEP)] = rest.astype(state.dtype)


def state_get(state, i, chunk):
    return (
        state[i, 0, pl.ds(STEP * chunk, STEP)].astype(jnp.float32),
        state[i, 1, pl.ds(STEP * chunk, STEP)].astype(jnp.float32),
    )


def halo_in(wire, target, keep):
    cols = target.shape[1] - 2

    def frame_body(frame):
        each_chunk(cols, lambda chunk: store_pieces(target, frame, chunk, *unpack_wire(wire, frame, chunk, keep)))

    each_frame(HALO, frame_body)


def second_kernel(
    starts, frames, dense_halo, dense, gains, weight, first_in, second_in, first, second, third, state, wire, hidden, gain_pad
):
    cols = first.shape[1] - 2
    channels = gains.shape[1]
    keep = keep_factor(starts, frames)
    fill_gain(gains, gain_pad)
    clear_borders(third)
    hidden[:, 1] = jnp.zeros_like(hidden[:, 1])

    def enter(frame):
        def body(chunk):
            main, rest = unpack_dense(dense_halo, frame, chunk)
            main, rest = activate(main, rest, *load_gain(gains, gain_pad, 0), channels)
            store_pieces(first, frame, chunk, main * keep, rest * keep)

        each_chunk(cols, body)

    each_frame(HALO, enter)
    hidden_out(first, 0, weight, 0, hidden, gains, gain_pad, 1, second, None)

    def finish(i, chunk, main, rest):
        main_in, rest_in = unpack_dense(dense, HALO + i, chunk)
        main, rest = rounded(main + main_in), rounded(rest + rest_in)
        state_put(state, i, chunk, main, rest)
        main, rest = activate(main, rest, *load_gain(gains, gain_pad, 2), channels)
        store_pieces(third, 2 * HALO + i, chunk, main, rest)
        pack_wire(wire, i, chunk, main, rest)

    residual_out(second, HALO, weight, 1, hidden, finish)


def third_kernel(
    starts, frames, halo, dense, gains, weight, second_in, third_in, second, third, fourth, state, wire, hidden, gain_pad
):
    channels = gains.shape[1]
    keep = keep_factor(starts, frames)
    fill_gain(gains, gain_pad)
    clear_borders(fourth)
    hidden[:, 1] = jnp.zeros_like(hidden[:, 1])
    halo_in(halo, second, keep)

    def finish(i, chunk, main, rest):
        main_in, rest_in = unpack_dense(dense, i, chunk)
        main, rest = rounded(main + main_in), rounded(rest + rest_in)
        state_put(state, i, chunk, main, rest)
        main, rest = activate(main, rest, *load_gain(gains, gain_pad, 2), channels)
        store_pieces(third, HALO + i, chunk, main, rest)

    residual_out(second, 0, weight, 1, hidden, finish)
    hidden_out(third, HALO, weight, 2, hidden, gains, gain_pad, 3, fourth, wire)


def live_factor(starts, frames, frame, span_frames):
    span, own_start, own_frames = own_span(starts, frames)
    return jnp.where((span - own_start) * span_frames + frame < own_frames, 1.0, 0.0).astype(jnp.float32)


def fourth_kernel(
    starts, frames, halo, gains, weight, third_in, fourth_in, state, third, fourth, out, hidden, gain_pad
):
    keep = keep_factor(starts, frames)
    fill_gain(gains, gain_pad)
    hidden[:, 1] = jnp.zeros_like(hidden[:, 1])
    halo_in(halo, third, keep)
    hidden_out(third, 0, weight, 2, hidden, gains, gain_pad, 3, fourth, None)

    def finish(i, chunk, main, rest):
        main_in, rest_in = state_get(state, i, chunk)
        live = live_factor(starts, frames, HALO + i, 2 * HALO)
        pack_dense(out, i, chunk, (main + main_in) * live, (rest + rest_in) * live)

    residual_out(fourth, HALO, weight, 3, hidden, finish)


def fifth_kernel(starts, frames, halo, weight, fourth_in, state, later, fourth, out, hidden):
    keep = keep_factor(starts, frames)
    hidden[:, 1] = jnp.zeros_like(hidden[:, 1])
    halo_in(halo, fourth, keep)
    out[HALO:] = later[...]

    def finish(i, chunk, main, rest):
        main_in, rest_in = state_get(state, i, chunk)
        live = live_factor(starts, frames, i, 2 * HALO)
        pack_dense(out, i, chunk, (main + main_in) * live, (rest + rest_in) * live)

    residual_out(fourth, 0, weight, 3, hidden, finish)


def local(features, gains, conv_weights, video_frames, video_start):
    frames, rows, merged = features.shape
    channels = gains.shape[1]
    cols = merged // channels
    layers = conv_weights.shape[0]
    weight = conv_weights.reshape(layers, 27, channels, channels)
    bf16, f32 = jnp.bfloat16, jnp.float32
    pieces = jax.ShapeDtypeStruct((frames + HALO, cols + 2, rows, 5 * LANES), bf16)
    wire = jax.ShapeDtypeStruct((HALO, cols * 3 // 2, rows, LANES), bf16)
    state = jax.ShapeDtypeStruct((HALO, 2, cols, rows, LANES), bf16)
    hidden = VMEM((2 * HALO, 2, cols, rows, LANES), f32)
    gain_pad = VMEM((layers, 2, LANES), f32)
    smem = pl.BlockSpec(memory_space=pltpu.SMEM)
    vmem = pl.BlockSpec(memory_space=VMEM)
    hbm = pl.BlockSpec(memory_space=pltpu.HBM)

    def call(body, ins, outs, scratch, convs, aliases=None, name=None):
        return pl.pallas_call(
            body,
            out_shape=outs,
            in_specs=ins,
            out_specs=tuple(vmem for _ in outs),
            scratch_shapes=scratch,
            input_output_aliases=aliases or {},
            name=name,
            compiler_params=pltpu.CompilerParams(vmem_limit_bytes=12 << 20),
            cost_estimate=pl.CostEstimate(
                flops=convs * 2 * 27 * channels * channels * rows * cols * 2,
                bytes_accessed=4 << 20,
                transcendentals=0,
            ),
        )

    halo0 = passed_along(features[frames - HALO :], "tm")
    first, second, wire1 = call(
        first_kernel,
        [hbm, hbm, hbm],
        (pieces, pieces, wire),
        [
            VMEM(features.shape, bf16),
            VMEM(gains.shape, f32),
            VMEM((1, 27, channels, channels), bf16),
            hidden,
            gain_pad,
            pltpu.SemaphoreType.DMA((3,)),
        ],
        1,
        name="k1",
    )(*(pltpu.with_memory_space_constraint(a, pltpu.HBM) for a in (features, gains, weight)))
    halo1 = passed_along(wire1, "tm")
    _, second, third, state_late, wire2 = call(
        second_kernel,
        [smem, smem] + [vmem] * 6,
        (pieces, pieces, pieces, state, wire),
        [hidden, gain_pad],
        2,
        {6: 0, 7: 1},
        name="k2",
    )(video_start, video_frames, halo0, features, gains, weight, first, second)
    halo2 = passed_along(wire2, "tm")
    _, third, fourth, state_early, wire3 = call(
        third_kernel,
        [smem, smem] + [vmem] * 6,
        (pieces, pieces, pieces, state, wire),
        [hidden, gain_pad],
        2,
        {6: 0, 7: 1},
        name="k3",
    )(video_start, video_frames, halo1, features, gains, weight, second, third)
    halo3 = passed_along(wire3, "tm")
    dense_half = jax.ShapeDtypeStruct((HALO, rows, merged), bf16)
    _, fourth, later = call(
        fourth_kernel,
        [smem, smem] + [vmem] * 6,
        (pieces, pieces, dense_half),
        [hidden, gain_pad],
        2,
        {5: 0, 6: 1},
        name="k4",
    )(video_start, video_frames, halo2, gains, weight, third, fourth, state_late)
    _, out = call(
        fifth_kernel,
        [smem, smem] + [vmem] * 5,
        (pieces, jax.ShapeDtypeStruct(features.shape, bf16)),
        [hidden],
        1,
        {4: 0},
        name="k5",
    )(video_start, video_frames, halo3, weight, fourth, state_early, later)
    return out


def solution(mesh):
    in_specs = (P(("grp", "tm"), None, None), P(), P(), P("grp"), P("grp"))
    out_specs = P(("grp", "tm"), None, None)
    return jax.shard_map(local, mesh=mesh, in_specs=in_specs, out_specs=out_specs, check_vma=False)
```

```python
import jax
import jax.numpy as jnp
from jax import lax
from jax.experimental import pallas as pl
from jax.experimental.pallas import tpu as pltpu
from jax.sharding import PartitionSpec as P


LANES = 128
HALO = 2
STEP = 4
STAGED = 1
OLD_FIRST = (0, 1, 2)
NEW_FIRST = (2, 1, 0)
WHOLE = (1, 1)
LAST_SPLIT = (1, 1)
VMEM = pltpu.VMEM


def passed_along(value, axis, swap_first):
    count = lax.axis_size(axis)
    swap = [(i, i ^ 1) for i in range(count)]
    cross = [(i, i + 1) for i in range(1, count - 1, 2)]
    orders = {"a": swap, "b": cross} if swap_first else {"a": cross, "b": swap}
    results = []
    for pairs in orders.values():
        results.append(lax.ppermute(value, axis, pairs))
    return tuple(results) if swap_first else tuple(results[::-1])


def received(swapped, crossed, index):
    odd = lax.rem(lax.axis_index("tm"), 2) == 1
    return jnp.where(odd, swapped[index].astype(jnp.float32), crossed[index].astype(jnp.float32))


def low_half(shape):
    return lax.broadcasted_iota(jnp.int32, shape, len(shape) - 1) < LANES // 2


def swap_half(value):
    return pltpu.roll(value, LANES // 2, axis=value.ndim - 1)


def activate(main, rest, gain_main, gain_rest, channels):
    total = jnp.sum(main * main + rest * rest, axis=-1, keepdims=True)
    inverse = lax.rsqrt(total * (1.0 / channels) + 1e-06)

    def silu(value, gain):
        scaled = value * inverse * gain
        half = 0.5 * scaled
        return half * jnp.tanh(half) + half

    return silu(main, gain_main), silu(rest, gain_rest)


def load_gain(gain_pad, index):
    return gain_pad[index, 0][None, None, :], gain_pad[index, 1][None, None, :]


def fill_gain(gains, gain_pad):
    count, channels = gains.shape
    gain_pad[...] = jnp.zeros_like(gain_pad)
    for k in range(count):
        gain_pad[k, 0:1, :] = gains[k : k + 1, 0:LANES]
        gain_pad[k, 1:2, 0 : channels - LANES] = gains[k : k + 1, LANES:channels]


def dense_chunk(frame, chunk):
    width = STEP * 192
    return (frame, slice(None), slice(chunk * width, (chunk + 1) * width))


def unpack_dense(block):
    rows, width = block.shape
    block = block.astype(jnp.float32)
    tile = [block[:, LANES * i : LANES * (i + 1)] for i in range(width // LANES)]
    low = low_half((rows, LANES))
    main, rest = [], []
    for i in range(0, len(tile), 3):
        rolled_b, rolled_c = swap_half(tile[i + 1]), swap_half(tile[i + 2])
        main += [tile[i], jnp.where(low, rolled_b, rolled_c)]
        rest += [jnp.where(low, tile[i + 1], 0.0), jnp.where(low, rolled_c, 0.0)]
    return jnp.stack(main), jnp.stack(rest)


def pack_dense(target, frame, chunk, main, rest):
    rows = target.shape[1]
    width = STEP * 192
    low = low_half((rows, LANES))
    tile = []
    for i in range(0, STEP, 2):
        rolled = swap_half(main[i + 1])
        tile += [main[i], jnp.where(low, rest[i], rolled), jnp.where(low, rolled, swap_half(rest[i + 1]))]
    block = jnp.concatenate(tile, axis=-1).astype(target.dtype)
    target[frame, :, chunk * width : (chunk + 1) * width] = block


def unpack_wire(read, cols, frame, chunk):
    main = read((frame, pl.ds(STEP * chunk, STEP)))
    pair = read((frame, pl.ds(cols + STEP // 2 * chunk, STEP // 2)))
    low = low_half(pair.shape)
    rest = jnp.stack([jnp.where(low, pair, 0.0), jnp.where(low, swap_half(pair), 0.0)], axis=1)
    return main, rest.reshape(main.shape)


def pack_wire(target, frame, chunk, main, rest):
    cols = target.shape[1] * 2 // 3
    target[frame, pl.ds(STEP * chunk, STEP)] = main.astype(target.dtype)
    pair = rest.reshape((STEP // 2, 2) + rest.shape[1:])
    target[frame, pl.ds(cols + STEP // 2 * chunk, STEP // 2)] = (pair[:, 0] + swap_half(pair[:, 1])).astype(target.dtype)


def clear_borders(buf):
    frames, slots, rows, lanes = buf.shape
    for frame in range(frames):
        for slot in (0, slots - 2, slots - 1):
            buf[frame, slot] = jnp.zeros((rows, lanes), buf.dtype)


def store_pieces(buf, frame, chunk, main, rest):
    rows = main.shape[1]
    row = lax.broadcasted_iota(jnp.int32, main.shape, 1)

    def above(value):
        return jnp.where(row == 0, 0.0, pltpu.roll(value, 1, axis=1))

    def below(value):
        return jnp.where(row == rows - 1, 0.0, pltpu.roll(value, rows - 1, axis=1))

    def put(first_slot, lane, value):
        buf[frame, pl.ds(first_slot, STEP), :, lane : lane + value.shape[-1]] = value.astype(buf.dtype)

    slot = STEP * chunk + 1
    put(slot, 0, above(main))
    put(slot, LANES, main)
    put(slot, 2 * LANES, below(main))
    put(slot, 3 * LANES, above(rest) + swap_half(rest))
    lower = below(rest)
    put(slot, 4 * LANES, lower[..., : LANES // 2])
    put(slot - 1, 4 * LANES + LANES // 2, lower[..., : LANES // 2])


def convolve(buf, frame, weight, hidden, slot, first_col, cols, taps):
    rows = buf.shape[2]
    channels = weight.shape[-1]
    span = channels - LANES

    def piece(tap, col, lane):
        return buf[frame + tap, first_col + col : first_col + col + cols, :, lane : lane + LANES].reshape(cols * rows, LANES)

    def taken(tap, row, col, rest):
        index = (tap * 3 + row) * 3 + col
        return weight[index, LANES:channels, :] if rest else weight[index, 0:LANES, :]

    lhs, rhs = [], []
    for tap in taps:
        for col in range(3):
            for row in range(3):
                lhs.append(piece(tap, col, LANES * row))
                rhs.append(taken(tap, row, col, False))
            lhs.append(piece(tap, col, 3 * LANES))
            rhs += [taken(tap, 0, col, True), taken(tap, 1, col, True)]
        lhs.append(piece(tap, 0, 4 * LANES))
        rhs += [taken(tap, 2, 0, True), taken(tap, 2, 1, True)]
        lhs.append(piece(tap, 2, 4 * LANES))
        rhs += [taken(tap, 2, 2, True), jnp.zeros((span, channels), weight.dtype)]
    total = jnp.dot(jnp.concatenate(lhs, axis=1), jnp.concatenate(rhs, axis=0), preferred_element_type=jnp.float32)
    hidden[slot, 0, first_col : first_col + cols] = total[:, :LANES].reshape(cols, rows, LANES)
    hidden[slot, 1, first_col : first_col + cols, :, 0:span] = total[:, LANES:].reshape(cols, rows, span)


def each_chunk(cols, body):
    for chunk in range(cols // STEP):
        body(chunk)


def each_frame(count, body):
    for index in range(count):
        body(index)


def hidden_chunk(hidden, slot, chunk):
    return hidden[slot, 0, pl.ds(STEP * chunk, STEP)], hidden[slot, 1, pl.ds(STEP * chunk, STEP)]


def own_span(starts, frames):
    span = lax.axis_index("tm")
    own_start, own_frames = starts[0], frames[0]
    for v in range(1, starts.shape[0]):
        here = starts[v] <= span
        own_start = jnp.where(here, starts[v], own_start)
        own_frames = jnp.where(here, frames[v], own_frames)
    return span, own_start, own_frames


def keep_factor(starts, frames):
    span, own_start, _ = own_span(starts, frames)
    return jnp.where(span - 1 >= own_start, 1.0, 0.0).astype(jnp.float32)


def stage_kernel(dense_hbm, gains_hbm, weight_hbm, first, wire, dense, weight, gains, gain_pad, sems):
    copies = [
        pltpu.make_async_copy(dense_hbm, dense, sems.at[0]),
        pltpu.make_async_copy(gains_hbm, gains, sems.at[1]),
        pltpu.make_async_copy(dense_hbm.at[pl.ds(HALO, HALO)], wire, sems.at[2]),
        pltpu.make_async_copy(weight_hbm.at[pl.ds(0, 1)], weight, sems.at[3]),
    ]
    for copy in copies:
        copy.start()
    clear_borders(first)
    for copy in copies[:3]:
        copy.wait()
    fill_gain(gains, gain_pad)
    for frame in range(STAGED):
        dense_in(dense, first, frame, gains, gain_pad)
    copies[3].wait()


def dense_in(dense, first, frame, gains, gain_pad):
    channels = gains.shape[1]

    def body(chunk):
        main, rest = unpack_dense(dense[dense_chunk(frame, chunk)])
        main, rest = activate(main, rest, *load_gain(gain_pad, 0), channels)
        store_pieces(first, frame + HALO, chunk, main, rest)

    each_chunk(first.shape[1] - 2, body)


def first_kernel(dense, gains, weight, weight_hbm, first_in, first, wire, later_weight, hidden, gain_pad, sem):
    copy = pltpu.make_async_copy(weight_hbm.at[pl.ds(1, later_weight.shape[0])], later_weight, sem)
    copy.start()
    fill_gain(gains, gain_pad)
    hidden[:, 1] = jnp.zeros_like(hidden[:, 1])
    for frame in range(STAGED, dense.shape[0]):
        dense_in(dense, first, frame, gains, gain_pad)
    hidden_out(first, HALO, weight.at[0], 0, hidden, gains, gain_pad, 1, None, wire, OLD_FIRST, LAST_SPLIT)
    copy.wait()


def convolve_frames(source, base, weight, layer, hidden, taps, splits, finish):
    cols = source.shape[1] - 2
    for i in range(HALO):
        part = cols // splits[i]
        for first_col in range(0, cols, part):
            slot = 2 * (layer % 2) + i
            convolve(source, base + i, weight, hidden, slot, first_col, part, taps)
            for chunk in range(first_col // STEP, (first_col + part) // STEP):
                finish(i, chunk, *hidden_chunk(hidden, slot, chunk))


def hidden_out(source, base, weight, layer, hidden, gains, gain_pad, gain_index, target, wire, taps, splits):
    channels = gains.shape[1]

    def finish(i, chunk, main, rest):
        main, rest = activate(main, rest, *load_gain(gain_pad, gain_index), channels)
        if wire is None:
            store_pieces(target, base + HALO + i, chunk, main, rest)
        else:
            pack_wire(wire, i, chunk, main, rest)

    convolve_frames(source, base, weight, layer, hidden, taps, splits, finish)


def residual_out(source, base, weight, layer, hidden, taps, splits, finish):
    convolve_frames(source, base, weight, layer, hidden, taps, splits, finish)


def rounded(value):
    return value.astype(jnp.bfloat16).astype(jnp.float32)


def state_put(state, i, chunk, main, rest):
    state[i, 0, pl.ds(STEP * chunk, STEP)] = main.astype(state.dtype)
    state[i, 1, pl.ds(STEP * chunk, STEP)] = rest.astype(state.dtype)


def state_get(state, i, chunk):
    return (
        state[i, 0, pl.ds(STEP * chunk, STEP)].astype(jnp.float32),
        state[i, 1, pl.ds(STEP * chunk, STEP)].astype(jnp.float32),
    )


def wire_in(read, target, base):
    cols = target.shape[1] - 2
    for frame in range(HALO):
        each_chunk(cols, lambda chunk: store_pieces(target, base + frame, chunk, *unpack_wire(read, cols, frame, chunk)))


def halo_in(swapped, crossed, target, keep):
    wire_in(lambda index: received(swapped, crossed, index) * keep, target, 0)


def own_in(wire, target):
    wire_in(lambda index: wire[index].astype(jnp.float32), target, 2 * HALO)


def second_kernel(
    starts, frames, swapped, crossed, dense, gains, own, weight, later_weight, first_in, first, second, state, wire, hidden, gain_pad
):
    cols = first.shape[1] - 2
    channels = gains.shape[1]
    keep = keep_factor(starts, frames)
    fill_gain(gains, gain_pad)
    clear_borders(second)
    own_in(own, second)
    hidden[:, 1] = jnp.zeros_like(hidden[:, 1])

    def enter(frame):
        def body(chunk):
            main, rest = unpack_dense(received(swapped, crossed, dense_chunk(frame, chunk)))
            main, rest = activate(main, rest, *load_gain(gain_pad, 0), channels)
            store_pieces(first, frame, chunk, main * keep, rest * keep)

        each_chunk(cols, body)

    each_frame(HALO, enter)
    hidden_out(first, 0, weight.at[0], 0, hidden, gains, gain_pad, 1, second, None, NEW_FIRST, WHOLE)

    def finish(i, chunk, main, rest):
        main_in, rest_in = unpack_dense(dense[dense_chunk(HALO + i, chunk)])
        main, rest = rounded(main + main_in), rounded(rest + rest_in)
        state_put(state, i, chunk, main, rest)
        main, rest = activate(main, rest, *load_gain(gain_pad, 2), channels)
        pack_wire(wire, i, chunk, main, rest)

    residual_out(second, HALO, later_weight.at[0], 1, hidden, NEW_FIRST, LAST_SPLIT, finish)


def third_kernel(
    starts, frames, swapped, crossed, dense, gains, own, later_weight, second_in, second, third, state, wire, hidden, gain_pad
):
    channels = gains.shape[1]
    keep = keep_factor(starts, frames)
    fill_gain(gains, gain_pad)
    clear_borders(third)
    own_in(own, third)
    hidden[:, 1] = jnp.zeros_like(hidden[:, 1])
    halo_in(swapped, crossed, second, keep)

    def finish(i, chunk, main, rest):
        main_in, rest_in = unpack_dense(dense[dense_chunk(i, chunk)])
        main, rest = rounded(main + main_in), rounded(rest + rest_in)
        state_put(state, i, chunk, main, rest)
        main, rest = activate(main, rest, *load_gain(gain_pad, 2), channels)
        store_pieces(third, HALO + i, chunk, main, rest)

    residual_out(second, 0, later_weight.at[0], 1, hidden, NEW_FIRST, WHOLE, finish)
    hidden_out(third, HALO, later_weight.at[1], 2, hidden, gains, gain_pad, 3, None, wire, NEW_FIRST, LAST_SPLIT)


def live_factor(starts, frames, frame, span_frames):
    span, own_start, own_frames = own_span(starts, frames)
    return jnp.where((span - own_start) * span_frames + frame < own_frames, 1.0, 0.0).astype(jnp.float32)


def fourth_kernel(
    starts, frames, swapped, crossed, gains, own, later_weight, third_in, state, third, fourth, out, hidden, gain_pad
):
    keep = keep_factor(starts, frames)
    fill_gain(gains, gain_pad)
    clear_borders(fourth)
    own_in(own, fourth)
    hidden[:, 1] = jnp.zeros_like(hidden[:, 1])
    halo_in(swapped, crossed, third, keep)
    hidden_out(third, 0, later_weight.at[1], 2, hidden, gains, gain_pad, 3, fourth, None, NEW_FIRST, WHOLE)

    def finish(i, chunk, main, rest):
        main_in, rest_in = state_get(state, i, chunk)
        live = live_factor(starts, frames, HALO + i, 2 * HALO)
        pack_dense(out, i, chunk, (main + main_in) * live, (rest + rest_in) * live)

    residual_out(fourth, HALO, later_weight.at[2], 3, hidden, NEW_FIRST, LAST_SPLIT, finish)


def fifth_kernel(
    starts, frames, swapped, crossed, later_weight, fourth_in, state, later, fourth, out, hidden, stage, sems
):
    keep = keep_factor(starts, frames)
    copies = [pltpu.make_async_copy(later, out.at[pl.ds(HALO, HALO)], sems.at[0])]
    copies[0].start()
    hidden[:, 1] = jnp.zeros_like(hidden[:, 1])
    halo_in(swapped, crossed, fourth, keep)

    def finish(i, chunk, main, rest):
        main_in, rest_in = state_get(state, i, chunk)
        live = live_factor(starts, frames, i, 2 * HALO)
        pack_dense(stage, i, chunk, (main + main_in) * live, (rest + rest_in) * live)

    residual_out(fourth, 0, later_weight.at[2], 3, hidden, NEW_FIRST, LAST_SPLIT, finish)
    for i in range(HALO):
        copies.append(pltpu.make_async_copy(stage.at[i], out.at[i], sems.at[1 + i]))
        copies[-1].start()
    for copy in copies:
        copy.wait()


def local(features, gains, conv_weights, video_frames, video_start):
    frames, rows, merged = features.shape
    channels = gains.shape[1]
    cols = merged // channels
    layers = conv_weights.shape[0]
    weight = conv_weights.reshape(layers, 27, channels, channels)
    bf16, f32 = jnp.bfloat16, jnp.float32
    pieces = jax.ShapeDtypeStruct((frames + HALO, cols + 2, rows, 5 * LANES), bf16)
    wire = jax.ShapeDtypeStruct((HALO, cols * 3 // 2, rows, LANES), bf16)
    state = jax.ShapeDtypeStruct((HALO, 2, cols, rows, LANES), bf16)
    hidden = VMEM((2 * HALO, 2, cols, rows, LANES), f32)
    gain_pad = VMEM((layers, 2, LANES), f32)
    smem = pl.BlockSpec(memory_space=pltpu.SMEM)
    vmem = pl.BlockSpec(memory_space=VMEM)
    hbm = pl.BlockSpec(memory_space=pltpu.HBM)

    def call(body, ins, outs, scratch, convs, aliases=None, out_specs=None):
        return pl.pallas_call(
            body,
            out_shape=outs,
            in_specs=ins,
            out_specs=out_specs or tuple(vmem for _ in outs),
            scratch_shapes=scratch,
            input_output_aliases=aliases or {},
            compiler_params=pltpu.CompilerParams(vmem_limit_bytes=12 << 20),
            cost_estimate=pl.CostEstimate(
                flops=convs * 2 * 27 * channels * channels * rows * cols * 2,
                bytes_accessed=4 << 20,
                transcendentals=0,
            ),
        )

    def weights(count):
        return jax.ShapeDtypeStruct((count, 27, channels, channels), bf16)

    dense = jax.ShapeDtypeStruct(features.shape, bf16)
    dense_half = jax.ShapeDtypeStruct((HALO, rows, merged), bf16)
    dma = pltpu.SemaphoreType.DMA
    features_hbm, gains_hbm, weight_hbm = (
        pltpu.with_memory_space_constraint(a, pltpu.HBM) for a in (features, gains, weight)
    )
    scalars = (video_start, video_frames)

    first, wire0, features, weight0 = call(
        stage_kernel,
        [hbm, hbm, hbm],
        (pieces, dense_half, dense, weights(1)),
        [VMEM(gains.shape, f32), gain_pad, dma((4,))],
        0,
    )(features_hbm, gains_hbm, weight_hbm)
    halo0 = passed_along(wire0, "tm", True)
    first, wire1, later_weight = call(
        first_kernel,
        [vmem, vmem, vmem, hbm, vmem],
        (pieces, wire, weights(layers - 1)),
        [hidden, gain_pad, dma],
        1,
        {4: 0},
    )(features, gains, weight0, weight_hbm, first)
    halo1 = passed_along(wire1, "tm", False)
    _, second, state_late, wire2 = call(
        second_kernel, [smem, smem] + [vmem] * 8, (pieces, pieces, state, wire), [hidden, gain_pad], 2, {9: 0}
    )(*scalars, *halo0, features, gains, wire1, weight0, later_weight, first)
    halo2 = passed_along(wire2, "tm", True)
    _, third, state_early, wire3 = call(
        third_kernel, [smem, smem] + [vmem] * 7, (pieces, pieces, state, wire), [hidden, gain_pad], 2, {8: 0}
    )(*scalars, *halo1, features, gains, wire2, later_weight, second)
    halo3 = passed_along(wire3, "tm", False)
    _, fourth, later = call(
        fourth_kernel, [smem, smem] + [vmem] * 7, (pieces, pieces, dense_half), [hidden, gain_pad], 2, {7: 0}
    )(*scalars, *halo2, gains, wire3, later_weight, third, state_late)
    _, out = call(
        fifth_kernel,
        [smem, smem] + [vmem] * 6,
        (pieces, dense),
        [hidden, VMEM(dense_half.shape, bf16), dma((1 + HALO,))],
        1,
        {5: 0},
        (vmem, hbm),
    )(*scalars, *halo3, later_weight, fourth, state_early, later)
    return out


def solution(mesh):
    in_specs = (P(("grp", "tm"), None, None), P(), P(), P("grp"), P("grp"))
    out_specs = P(("grp", "tm"), None, None)
    return jax.shard_map(local, mesh=mesh, in_specs=in_specs, out_specs=out_specs, check_vma=False)
```

```python
import jax
import jax.numpy as jnp
from jax import lax
from jax.experimental import pallas as pl
from jax.experimental.pallas import tpu as pltpu
from jax.sharding import PartitionSpec as P


LANES = 128
HALO = 2
STEP = 4
STAGED = 1
OLD_FIRST = (0, 1, 2)
NEW_FIRST = (2, 1, 0)
WHOLE = (1, 1)
LAST_SPLIT = (1, 1)
VMEM = pltpu.VMEM


def is_odd():
    return lax.rem(lax.axis_index("tm"), 2) == 1


def plain(ref):
    return lambda index: ref[index].astype(jnp.float32)


def by_place(even_ref, odd_ref):
    odd = is_odd()
    return lambda index: jnp.where(odd, odd_ref[index].astype(jnp.float32), even_ref[index].astype(jnp.float32))


def at_place(body, odd, inputs, carried):
    def kernel(*refs):
        @pl.when(is_odd() == odd)
        def _():
            body(*refs[:inputs], *refs[inputs + carried :])

    return kernel


def low_half(shape):
    return lax.broadcasted_iota(jnp.int32, shape, len(shape) - 1) < LANES // 2


def swap_half(value):
    return pltpu.roll(value, LANES // 2, axis=value.ndim - 1)


def activate(main, rest, gain_main, gain_rest, channels):
    total = jnp.sum(main * main + rest * rest, axis=-1, keepdims=True)
    inverse = lax.rsqrt(total * (1.0 / channels) + 1e-06)

    def silu(value, gain):
        scaled = value * inverse * gain
        half = 0.5 * scaled
        return half * jnp.tanh(half) + half

    return silu(main, gain_main), silu(rest, gain_rest)


def load_gain(gain_pad, index):
    return gain_pad[index, 0][None, None, :], gain_pad[index, 1][None, None, :]


def fill_gain(gains, gain_pad):
    count, channels = gains.shape
    gain_pad[...] = jnp.zeros_like(gain_pad)
    for k in range(count):
        gain_pad[k, 0:1, :] = gains[k : k + 1, 0:LANES]
        gain_pad[k, 1:2, 0 : channels - LANES] = gains[k : k + 1, LANES:channels]


def dense_chunk(frame, chunk):
    width = STEP * 192
    return (frame, slice(None), slice(chunk * width, (chunk + 1) * width))


def unpack_dense(block):
    rows, width = block.shape
    block = block.astype(jnp.float32)
    tile = [block[:, LANES * i : LANES * (i + 1)] for i in range(width // LANES)]
    low = low_half((rows, LANES))
    main, rest = [], []
    for i in range(0, len(tile), 3):
        rolled_b, rolled_c = swap_half(tile[i + 1]), swap_half(tile[i + 2])
        main += [tile[i], jnp.where(low, rolled_b, rolled_c)]
        rest += [jnp.where(low, tile[i + 1], 0.0), jnp.where(low, rolled_c, 0.0)]
    return jnp.stack(main), jnp.stack(rest)


def pack_dense(target, frame, chunk, main, rest):
    rows = target.shape[1]
    width = STEP * 192
    low = low_half((rows, LANES))
    tile = []
    for i in range(0, STEP, 2):
        rolled = swap_half(main[i + 1])
        tile += [main[i], jnp.where(low, rest[i], rolled), jnp.where(low, rolled, swap_half(rest[i + 1]))]
    block = jnp.concatenate(tile, axis=-1).astype(target.dtype)
    target[frame, :, chunk * width : (chunk + 1) * width] = block


def unpack_wire(read, cols, frame, chunk):
    main = read((frame, pl.ds(STEP * chunk, STEP)))
    pair = read((frame, pl.ds(cols + STEP // 2 * chunk, STEP // 2)))
    low = low_half(pair.shape)
    rest = jnp.stack([jnp.where(low, pair, 0.0), jnp.where(low, swap_half(pair), 0.0)], axis=1)
    return main, rest.reshape(main.shape)


def pack_wire(target, frame, chunk, main, rest):
    cols = target.shape[1] * 2 // 3
    target[frame, pl.ds(STEP * chunk, STEP)] = main.astype(target.dtype)
    pair = rest.reshape((STEP // 2, 2) + rest.shape[1:])
    target[frame, pl.ds(cols + STEP // 2 * chunk, STEP // 2)] = (pair[:, 0] + swap_half(pair[:, 1])).astype(target.dtype)


def clear_borders(buf):
    frames, slots, rows, lanes = buf.shape
    for frame in range(frames):
        for slot in (0, slots - 2, slots - 1):
            buf[frame, slot] = jnp.zeros((rows, lanes), buf.dtype)


def store_pieces(buf, frame, chunk, main, rest):
    rows = main.shape[1]
    row = lax.broadcasted_iota(jnp.int32, main.shape, 1)

    def above(value):
        return jnp.where(row == 0, 0.0, pltpu.roll(value, 1, axis=1))

    def below(value):
        return jnp.where(row == rows - 1, 0.0, pltpu.roll(value, rows - 1, axis=1))

    def put(first_slot, lane, value):
        buf[frame, pl.ds(first_slot, STEP), :, lane : lane + value.shape[-1]] = value.astype(buf.dtype)

    slot = STEP * chunk + 1
    put(slot, 0, above(main))
    put(slot, LANES, main)
    put(slot, 2 * LANES, below(main))
    put(slot, 3 * LANES, above(rest) + swap_half(rest))
    lower = below(rest)
    put(slot, 4 * LANES, lower[..., : LANES // 2])
    put(slot - 1, 4 * LANES + LANES // 2, lower[..., : LANES // 2])


def convolve(buf, frame, weight, hidden, slot, first_col, cols, taps):
    rows = buf.shape[2]
    channels = weight.shape[-1]
    span = channels - LANES

    def piece(tap, col, lane):
        return buf[frame + tap, first_col + col : first_col + col + cols, :, lane : lane + LANES].reshape(cols * rows, LANES)

    def taken(tap, row, col, rest):
        index = (tap * 3 + row) * 3 + col
        return weight[index, LANES:channels, :] if rest else weight[index, 0:LANES, :]

    lhs, rhs = [], []
    for tap in taps:
        for col in range(3):
            for row in range(3):
                lhs.append(piece(tap, col, LANES * row))
                rhs.append(taken(tap, row, col, False))
            lhs.append(piece(tap, col, 3 * LANES))
            rhs += [taken(tap, 0, col, True), taken(tap, 1, col, True)]
        lhs.append(piece(tap, 0, 4 * LANES))
        rhs += [taken(tap, 2, 0, True), taken(tap, 2, 1, True)]
        lhs.append(piece(tap, 2, 4 * LANES))
        rhs += [taken(tap, 2, 2, True), jnp.zeros((span, channels), weight.dtype)]
    total = jnp.dot(jnp.concatenate(lhs, axis=1), jnp.concatenate(rhs, axis=0), preferred_element_type=jnp.float32)
    hidden[slot, 0, first_col : first_col + cols] = total[:, :LANES].reshape(cols, rows, LANES)
    hidden[slot, 1, first_col : first_col + cols, :, 0:span] = total[:, LANES:].reshape(cols, rows, span)


def each_chunk(cols, body):
    for chunk in range(cols // STEP):
        body(chunk)


def each_frame(count, body):
    for index in range(count):
        body(index)


def hidden_chunk(hidden, slot, chunk):
    return hidden[slot, 0, pl.ds(STEP * chunk, STEP)], hidden[slot, 1, pl.ds(STEP * chunk, STEP)]


def own_span(starts, frames):
    span = lax.axis_index("tm")
    own_start, own_frames = starts[0], frames[0]
    for v in range(1, starts.shape[0]):
        here = starts[v] <= span
        own_start = jnp.where(here, starts[v], own_start)
        own_frames = jnp.where(here, frames[v], own_frames)
    return span, own_start, own_frames


def stage_kernel(
    dense_hbm, gains_hbm, weight_hbm, starts_hbm, frames_hbm, first, wire, dense, weight, gain_pad, facts, gains, starts, frames, sems
):
    copies = [
        pltpu.make_async_copy(dense_hbm, dense, sems.at[0]),
        pltpu.make_async_copy(gains_hbm, gains, sems.at[1]),
        pltpu.make_async_copy(dense_hbm.at[pl.ds(HALO, HALO)], wire, sems.at[2]),
        pltpu.make_async_copy(starts_hbm, starts, sems.at[3]),
        pltpu.make_async_copy(frames_hbm, frames, sems.at[4]),
        pltpu.make_async_copy(weight_hbm.at[pl.ds(0, 1)], weight, sems.at[5]),
    ]
    for copy in copies:
        copy.start()
    clear_borders(first)
    for copy in copies[:5]:
        copy.wait()
    fill_gain(gains, gain_pad)
    span, own_start, own_frames = own_span(starts, frames)
    factors = [jnp.where(span - 1 >= own_start, 1.0, 0.0)]
    for frame in range(2 * HALO):
        factors.append(jnp.where((span - own_start) * (2 * HALO) + frame < own_frames, 1.0, 0.0))
    for row, factor in enumerate(factors):
        facts[row] = jnp.full((LANES,), factor, facts.dtype)
    for frame in range(STAGED):
        dense_in(dense, first, frame, gain_pad, gains.shape[1])
    copies[5].wait()


def dense_in(dense, first, frame, gain_pad, channels):
    def body(chunk):
        main, rest = unpack_dense(dense[dense_chunk(frame, chunk)])
        main, rest = activate(main, rest, *load_gain(gain_pad, 0), channels)
        store_pieces(first, frame + HALO, chunk, main, rest)

    each_chunk(first.shape[1] - 2, body)


def first_kernel(dense, gain_pad, weight, weight_hbm, first, wire, later_weight, hidden, sem):
    copy = pltpu.make_async_copy(weight_hbm.at[pl.ds(1, later_weight.shape[0])], later_weight, sem)
    copy.start()
    hidden[:, 1] = jnp.zeros_like(hidden[:, 1])
    for frame in range(STAGED, dense.shape[0]):
        dense_in(dense, first, frame, gain_pad, weight.shape[-1])
    hidden_out(first, HALO, weight.at[0], 0, hidden, gain_pad, 1, None, wire, OLD_FIRST, LAST_SPLIT)
    copy.wait()


def convolve_frames(source, base, weight, layer, hidden, taps, splits, finish):
    cols = source.shape[1] - 2
    for i in range(HALO):
        part = cols // splits[i]
        for first_col in range(0, cols, part):
            slot = 2 * (layer % 2) + i
            convolve(source, base + i, weight, hidden, slot, first_col, part, taps)
            for chunk in range(first_col // STEP, (first_col + part) // STEP):
                finish(i, chunk, *hidden_chunk(hidden, slot, chunk))


def hidden_out(source, base, weight, layer, hidden, gain_pad, gain_index, target, wire, taps, splits):
    channels = weight.shape[-1]

    def finish(i, chunk, main, rest):
        main, rest = activate(main, rest, *load_gain(gain_pad, gain_index), channels)
        if wire is None:
            store_pieces(target, base + HALO + i, chunk, main, rest)
        else:
            pack_wire(wire, i, chunk, main, rest)

    convolve_frames(source, base, weight, layer, hidden, taps, splits, finish)


def residual_out(source, base, weight, layer, hidden, taps, splits, finish):
    convolve_frames(source, base, weight, layer, hidden, taps, splits, finish)


def rounded(value):
    return value.astype(jnp.bfloat16).astype(jnp.float32)


def state_put(state, i, chunk, main, rest):
    state[i, 0, pl.ds(STEP * chunk, STEP)] = main.astype(state.dtype)
    state[i, 1, pl.ds(STEP * chunk, STEP)] = rest.astype(state.dtype)


def state_get(state, i, chunk):
    return (
        state[i, 0, pl.ds(STEP * chunk, STEP)].astype(jnp.float32),
        state[i, 1, pl.ds(STEP * chunk, STEP)].astype(jnp.float32),
    )


def wire_in(read, target, base):
    cols = target.shape[1] - 2
    for frame in range(HALO):
        each_chunk(cols, lambda chunk: store_pieces(target, base + frame, chunk, *unpack_wire(read, cols, frame, chunk)))


def halo_in(read, target, keep):
    wire_in(lambda index: read(index) * keep, target, 0)


def own_in(read, target):
    wire_in(read, target, 2 * HALO)


def second_kernel(
    facts, halo, dense, gain_pad, own, weight, later_weight, first, second, state, wire, hidden
):
    cols = first.shape[1] - 2
    channels = later_weight.shape[-1]
    keep = facts[0][None, None, :]
    clear_borders(second)
    own_in(plain(own), second)
    hidden[:, 1] = jnp.zeros_like(hidden[:, 1])

    def enter(frame):
        def body(chunk):
            main, rest = unpack_dense(halo[dense_chunk(frame, chunk)])
            main, rest = activate(main, rest, *load_gain(gain_pad, 0), channels)
            store_pieces(first, frame, chunk, main * keep, rest * keep)

        each_chunk(cols, body)

    each_frame(HALO, enter)
    hidden_out(first, 0, weight.at[0], 0, hidden, gain_pad, 1, second, None, NEW_FIRST, WHOLE)

    def finish(i, chunk, main, rest):
        main_in, rest_in = unpack_dense(dense[dense_chunk(HALO + i, chunk)])
        main, rest = rounded(main + main_in), rounded(rest + rest_in)
        state_put(state, i, chunk, main, rest)
        main, rest = activate(main, rest, *load_gain(gain_pad, 2), channels)
        pack_wire(wire, i, chunk, main, rest)

    residual_out(second, HALO, later_weight.at[0], 1, hidden, NEW_FIRST, LAST_SPLIT, finish)


def third_kernel(
    facts, halo, dense, gain_pad, own, later_weight, second, third, state, wire, hidden
):
    channels = later_weight.shape[-1]
    keep = facts[0][None, None, :]
    clear_borders(third)
    own_in(plain(own), third)
    hidden[:, 1] = jnp.zeros_like(hidden[:, 1])
    halo_in(plain(halo), second, keep)

    def finish(i, chunk, main, rest):
        main_in, rest_in = unpack_dense(dense[dense_chunk(i, chunk)])
        main, rest = rounded(main + main_in), rounded(rest + rest_in)
        state_put(state, i, chunk, main, rest)
        main, rest = activate(main, rest, *load_gain(gain_pad, 2), channels)
        store_pieces(third, HALO + i, chunk, main, rest)

    residual_out(second, 0, later_weight.at[0], 1, hidden, NEW_FIRST, WHOLE, finish)
    hidden_out(third, HALO, later_weight.at[1], 2, hidden, gain_pad, 3, None, wire, NEW_FIRST, LAST_SPLIT)


def fourth_kernel(
    facts, swapped, crossed, gain_pad, own_odd, own_even, later_weight, third_in, state, third, fourth, out, hidden
):
    keep = facts[0][None, None, :]
    clear_borders(fourth)
    own_in(by_place(own_even, own_odd), fourth)
    hidden[:, 1] = jnp.zeros_like(hidden[:, 1])
    halo_in(by_place(crossed, swapped), third, keep)
    hidden_out(third, 0, later_weight.at[1], 2, hidden, gain_pad, 3, fourth, None, NEW_FIRST, WHOLE)

    def finish(i, chunk, main, rest):
        main_in, rest_in = state_get(state, i, chunk)
        live = facts[1 + HALO + i][None, None, :]
        pack_dense(out, i, chunk, (main + main_in) * live, (rest + rest_in) * live)

    residual_out(fourth, HALO, later_weight.at[2], 3, hidden, NEW_FIRST, LAST_SPLIT, finish)


def fifth_kernel(
    facts, swapped, crossed, later_weight, fourth_in, state, later, fourth, out, hidden, stage, sems
):
    keep = facts[0][None, None, :]
    copies = [pltpu.make_async_copy(later, out.at[pl.ds(HALO, HALO)], sems.at[0])]
    copies[0].start()
    hidden[:, 1] = jnp.zeros_like(hidden[:, 1])
    halo_in(by_place(crossed, swapped), fourth, keep)

    def finish(i, chunk, main, rest):
        main_in, rest_in = state_get(state, i, chunk)
        live = facts[1 + i][None, None, :]
        pack_dense(stage, i, chunk, (main + main_in) * live, (rest + rest_in) * live)

    residual_out(fourth, 0, later_weight.at[2], 3, hidden, NEW_FIRST, LAST_SPLIT, finish)
    for i in range(HALO):
        copies.append(pltpu.make_async_copy(stage.at[i], out.at[i], sems.at[1 + i]))
        copies[-1].start()
    for copy in copies:
        copy.wait()


def local(features, gains, conv_weights, video_frames, video_start):
    frames, rows, merged = features.shape
    channels = gains.shape[1]
    cols = merged // channels
    layers = conv_weights.shape[0]
    weight = conv_weights.reshape(layers, 27, channels, channels)
    bf16, f32 = jnp.bfloat16, jnp.float32
    pieces = jax.ShapeDtypeStruct((frames + HALO, cols + 2, rows, 5 * LANES), bf16)
    wire = jax.ShapeDtypeStruct((HALO, cols * 3 // 2, rows, LANES), bf16)
    state = jax.ShapeDtypeStruct((HALO, 2, cols, rows, LANES), bf16)
    hidden = VMEM((2 * HALO, 2, cols, rows, LANES), f32)
    vmem = pl.BlockSpec(memory_space=VMEM)
    hbm = pl.BlockSpec(memory_space=pltpu.HBM)

    def call(body, ins, outs, scratch, convs, aliases=None, out_specs=None):
        return pl.pallas_call(
            body,
            out_shape=outs,
            in_specs=ins,
            out_specs=out_specs or tuple(vmem for _ in outs),
            scratch_shapes=scratch,
            input_output_aliases=aliases or {},
            compiler_params=pltpu.CompilerParams(vmem_limit_bytes=12 << 20),
            cost_estimate=pl.CostEstimate(
                flops=convs * 2 * 27 * channels * channels * rows * cols * 2,
                bytes_accessed=4 << 20,
                transcendentals=0,
            ),
        )

    def weights(count):
        return jax.ShapeDtypeStruct((count, 27, channels, channels), bf16)

    dense = jax.ShapeDtypeStruct(features.shape, bf16)
    dense_half = jax.ShapeDtypeStruct((HALO, rows, merged), bf16)
    dma = pltpu.SemaphoreType.DMA
    facts = jax.ShapeDtypeStruct((8, LANES), f32)
    gain_rows = jax.ShapeDtypeStruct((layers, 2, LANES), f32)
    in_hbm = [
        pltpu.with_memory_space_constraint(a, pltpu.HBM)
        for a in (features, gains, weight, video_start, video_frames)
    ]
    weight_hbm = in_hbm[2]
    count = lax.axis_size("tm")
    swap = [(i, i ^ 1) for i in range(count)]
    cross = [(i, i + 1) for i in range(1, count - 1, 2)]

    def half(body, odd, ins, specs, carried, outs, scratch, convs):
        kernel = at_place(body, odd, len(ins), len(carried))
        aliases = {len(ins) + n: index for n, index in enumerate(carried)}
        arrays = (*ins, *carried.values())
        return call(kernel, specs + [vmem] * len(carried), outs, scratch, convs, aliases)(*arrays)

    def exchange(sent, even_step, swapped_of, next_step):
        crossed = lax.ppermute(sent, "tm", cross)
        even = even_step()
        swapped = lax.ppermute(even[swapped_of], "tm", swap)
        after = next_step(even, swapped)
        return crossed, swapped, even, after

    def stage(odd, carried):
        outs = (pieces, dense_half, dense, weights(1), gain_rows, facts)
        small = pltpu.SMEM(video_start.shape, jnp.int32)
        scratch = [VMEM(gains.shape, f32), small, small, dma((6,))]
        return half(stage_kernel, odd, in_hbm, [hbm] * 5, carried, outs, scratch, 0)

    def step1(odd, staged, carried):
        _, _, block, weight0, gain_rows, _ = staged
        return half(
            first_kernel,
            odd,
            (block, gain_rows, weight0, weight_hbm),
            [vmem, vmem, vmem, hbm],
            carried,
            (pieces, wire, weights(layers - 1)),
            [hidden, dma],
            1,
        )

    def step2(odd, known, halo, block, own, weight0, later_weight, carried):
        return half(
            second_kernel,
            odd,
            (known[1], halo, block, known[0], own, weight0, later_weight),
            [vmem] * 7,
            carried,
            (pieces, pieces, state, wire),
            [hidden],
            2,
        )

    def step3(odd, known, halo, block, own, later_weight, carried):
        return half(
            third_kernel,
            odd,
            (known[1], halo, block, known[0], own, later_weight),
            [vmem] * 6,
            carried,
            (pieces, pieces, state, wire),
            [hidden],
            2,
        )

    odd0 = stage(True, {})
    crossed0, swapped0, staged, odd1 = exchange(
        odd0[1],
        lambda: stage(False, {n: odd0[n] for n in (0, 2, 3, 4, 5)}),
        1,
        lambda staged, _: step1(True, staged, {0: staged[0]}),
    )
    block, weight0, known = staged[2], staged[3], staged[4:]
    crossed1, swapped1, even1, odd2 = exchange(
        odd1[1],
        lambda: step1(False, staged, {0: odd1[0], 2: odd1[2]}),
        1,
        lambda even, _: step2(True, known, swapped0, block, odd1[1], weight0, even[2], {0: even[0]}),
    )
    later_weight = even1[2]
    crossed2, swapped2, even2, odd3 = exchange(
        odd2[3],
        lambda: step2(
            False, known, crossed0, block, even1[1], weight0, later_weight, {0: odd2[0], 1: odd2[1], 2: odd2[2]}
        ),
        3,
        lambda even, _: step3(True, known, swapped1, block, odd2[3], later_weight, {0: even[1]}),
    )
    state_late = even2[2]

    def last_steps(even, swapped):
        third = even[1]
        return call(
            fourth_kernel, [vmem] * 9, (pieces, pieces, dense_half), [hidden], 2, {7: 0}
        )(known[1], swapped2, crossed2, known[0], odd3[3], even[3], later_weight, third, state_late)

    crossed3, swapped3, even3, (_, fourth, later) = exchange(
        odd3[3],
        lambda: step3(False, known, crossed1, block, even2[3], later_weight, {0: odd3[0], 1: odd3[1], 2: odd3[2]}),
        3,
        last_steps,
    )
    _, out = call(
        fifth_kernel,
        [vmem] * 7,
        (pieces, dense),
        [hidden, VMEM(dense_half.shape, bf16), dma((1 + HALO,))],
        1,
        {4: 0},
        (vmem, hbm),
    )(known[1], swapped3, crossed3, later_weight, fourth, even3[2], later)
    return out


def solution(mesh):
    in_specs = (P(("grp", "tm"), None, None), P(), P(), P("grp"), P("grp"))
    out_specs = P(("grp", "tm"), None, None)
    return jax.shard_map(local, mesh=mesh, in_specs=in_specs, out_specs=out_specs, check_vma=False)
```

```python
import jax
import jax.numpy as jnp
from jax import lax
from jax.experimental import pallas as pl
from jax.experimental.pallas import tpu as pltpu
from jax.sharding import PartitionSpec as P


LANES = 128
HALO = 2
STEP = 4
STAGED = 0
OLD_FIRST = (0, 1, 2)
NEW_FIRST = (2, 1, 0)
WHOLE = 1
LAST_SPLIT = 2
END_SPLIT = 2
VMEM = pltpu.VMEM


def is_odd():
    return lax.rem(lax.axis_index("tm"), 2) == 1


def plain(ref):
    return lambda index: ref[index].astype(jnp.float32)


def by_place(even_ref, odd_ref):
    odd = is_odd()
    return lambda index: jnp.where(odd, odd_ref[index].astype(jnp.float32), even_ref[index].astype(jnp.float32))


def at_place(body, odd, inputs, carried):
    def kernel(*refs):
        @pl.when(is_odd() == odd)
        def _():
            body(*refs[:inputs], *refs[inputs + carried :])

    return kernel


def low_half(shape):
    return lax.broadcasted_iota(jnp.int32, shape, len(shape) - 1) < LANES // 2


def swap_half(value):
    return pltpu.roll(value, LANES // 2, axis=value.ndim - 1)


def activate(main, rest, gain_main, gain_rest, channels):
    total = jnp.sum(main * main + rest * rest, axis=-1, keepdims=True)
    inverse = lax.rsqrt(total * (1.0 / channels) + 1e-06)

    def silu(value, gain):
        scaled = value * inverse * gain
        half = 0.5 * scaled
        return half * jnp.tanh(half) + half

    return silu(main, gain_main), silu(rest, gain_rest)


def load_gain(gain_pad, index):
    return gain_pad[index, 0][None, None, :], gain_pad[index, 1][None, None, :]


def fill_gain(gains, gain_pad):
    count, channels = gains.shape
    gain_pad[...] = jnp.zeros_like(gain_pad)
    for k in range(count):
        gain_pad[k, 0:1, :] = gains[k : k + 1, 0:LANES]
        gain_pad[k, 1:2, 0 : channels - LANES] = gains[k : k + 1, LANES:channels]


def dense_chunk(frame, chunk):
    width = STEP * 192
    return (frame, slice(None), slice(chunk * width, (chunk + 1) * width))


def unpack_dense(block):
    rows, width = block.shape
    block = block.astype(jnp.float32)
    tile = [block[:, LANES * i : LANES * (i + 1)] for i in range(width // LANES)]
    low = low_half((rows, LANES))
    main, rest = [], []
    for i in range(0, len(tile), 3):
        rolled_b, rolled_c = swap_half(tile[i + 1]), swap_half(tile[i + 2])
        main += [tile[i], jnp.where(low, rolled_b, rolled_c)]
        rest += [jnp.where(low, tile[i + 1], 0.0), jnp.where(low, rolled_c, 0.0)]
    return jnp.stack(main), jnp.stack(rest)


def pack_dense(target, frame, chunk, main, rest):
    rows = target.shape[1]
    width = STEP * 192
    low = low_half((rows, LANES))
    tile = []
    for i in range(0, STEP, 2):
        rolled = swap_half(main[i + 1])
        tile += [main[i], jnp.where(low, rest[i], rolled), jnp.where(low, rolled, swap_half(rest[i + 1]))]
    block = jnp.concatenate(tile, axis=-1).astype(target.dtype)
    target[frame, :, chunk * width : (chunk + 1) * width] = block


def unpack_wire(read, cols, frame, chunk):
    main = read((frame, pl.ds(STEP * chunk, STEP)))
    pair = read((frame, pl.ds(cols + STEP // 2 * chunk, STEP // 2)))
    low = low_half(pair.shape)
    rest = jnp.stack([jnp.where(low, pair, 0.0), jnp.where(low, swap_half(pair), 0.0)], axis=1)
    return main, rest.reshape(main.shape)


def pack_wire(target, frame, chunk, main, rest):
    cols = target.shape[1] * 2 // 3
    target[frame, pl.ds(STEP * chunk, STEP)] = main.astype(target.dtype)
    pair = rest.reshape((STEP // 2, 2) + rest.shape[1:])
    target[frame, pl.ds(cols + STEP // 2 * chunk, STEP // 2)] = (pair[:, 0] + swap_half(pair[:, 1])).astype(target.dtype)


def clear_borders(buf):
    frames, slots, rows, lanes = buf.shape
    for frame in range(frames):
        for slot in (0, slots - 2, slots - 1):
            buf[frame, slot] = jnp.zeros((rows, lanes), buf.dtype)


def store_pieces(buf, frame, chunk, main, rest):
    rows = main.shape[1]
    row = lax.broadcasted_iota(jnp.int32, main.shape, 1)

    def above(value):
        return jnp.where(row == 0, 0.0, pltpu.roll(value, 1, axis=1))

    def below(value):
        return jnp.where(row == rows - 1, 0.0, pltpu.roll(value, rows - 1, axis=1))

    def put(first_slot, lane, value):
        buf[frame, pl.ds(first_slot, STEP), :, lane : lane + value.shape[-1]] = value.astype(buf.dtype)

    slot = STEP * chunk + 1
    put(slot, 0, above(main))
    put(slot, LANES, main)
    put(slot, 2 * LANES, below(main))
    put(slot, 3 * LANES, above(rest) + swap_half(rest))
    lower = below(rest)
    put(slot, 4 * LANES, lower[..., : LANES // 2])
    put(slot - 1, 4 * LANES + LANES // 2, lower[..., : LANES // 2])


def convolve(buf, frame, weight, hidden, slot, first_col, cols, taps):
    rows = buf.shape[2]
    channels = weight.shape[-1]
    span = channels - LANES

    def piece(tap, col, lane):
        return buf[frame + tap, first_col + col : first_col + col + cols, :, lane : lane + LANES].reshape(cols * rows, LANES)

    def taken(tap, row, col, rest):
        index = (tap * 3 + row) * 3 + col
        return weight[index, LANES:channels, :] if rest else weight[index, 0:LANES, :]

    lhs, rhs = [], []
    for tap in taps:
        for col in range(3):
            for row in range(3):
                lhs.append(piece(tap, col, LANES * row))
                rhs.append(taken(tap, row, col, False))
            lhs.append(piece(tap, col, 3 * LANES))
            rhs += [taken(tap, 0, col, True), taken(tap, 1, col, True)]
        lhs.append(piece(tap, 0, 4 * LANES))
        rhs += [taken(tap, 2, 0, True), taken(tap, 2, 1, True)]
        lhs.append(piece(tap, 2, 4 * LANES))
        rhs += [taken(tap, 2, 2, True), jnp.zeros((span, channels), weight.dtype)]
    total = jnp.dot(jnp.concatenate(lhs, axis=1), jnp.concatenate(rhs, axis=0), preferred_element_type=jnp.float32)
    hidden[slot, 0, first_col : first_col + cols] = total[:, :LANES].reshape(cols, rows, LANES)
    hidden[slot, 1, first_col : first_col + cols, :, 0:span] = total[:, LANES:].reshape(cols, rows, span)


def each_chunk(cols, body):
    for chunk in range(cols // STEP):
        body(chunk)


def each_frame(count, body):
    for index in range(count):
        body(index)


def hidden_chunk(hidden, slot, chunk):
    return hidden[slot, 0, pl.ds(STEP * chunk, STEP)], hidden[slot, 1, pl.ds(STEP * chunk, STEP)]


def own_span(starts, frames):
    span = lax.axis_index("tm")
    own_start, own_frames = starts[0], frames[0]
    for v in range(1, starts.shape[0]):
        here = starts[v] <= span
        own_start = jnp.where(here, starts[v], own_start)
        own_frames = jnp.where(here, frames[v], own_frames)
    return span, own_start, own_frames


def stage_kernel(
    dense_hbm, gains_hbm, weight_hbm, starts_hbm, frames_hbm, first, wire, dense, weight, gain_pad, facts, gains, starts, frames, sems
):
    copies = [
        pltpu.make_async_copy(dense_hbm, dense, sems.at[0]),
        pltpu.make_async_copy(gains_hbm, gains, sems.at[1]),
        pltpu.make_async_copy(dense_hbm.at[pl.ds(HALO, HALO)], wire, sems.at[2]),
        pltpu.make_async_copy(starts_hbm, starts, sems.at[3]),
        pltpu.make_async_copy(frames_hbm, frames, sems.at[4]),
        pltpu.make_async_copy(weight_hbm.at[pl.ds(0, 1)], weight, sems.at[5]),
    ]
    for copy in copies:
        copy.start()
    clear_borders(first)
    for copy in copies[:5]:
        copy.wait()
    fill_gain(gains, gain_pad)
    span, own_start, own_frames = own_span(starts, frames)
    factors = [jnp.where(span - 1 >= own_start, 1.0, 0.0)]
    for frame in range(2 * HALO):
        factors.append(jnp.where((span - own_start) * (2 * HALO) + frame < own_frames, 1.0, 0.0))
    for row, factor in enumerate(factors):
        facts[row] = jnp.full((LANES,), factor, facts.dtype)
    for frame in range(STAGED):
        dense_in(dense, first, frame, gain_pad, gains.shape[1])
    copies[5].wait()


def dense_in(dense, first, frame, gain_pad, channels):
    def body(chunk):
        main, rest = unpack_dense(dense[dense_chunk(frame, chunk)])
        main, rest = activate(main, rest, *load_gain(gain_pad, 0), channels)
        store_pieces(first, frame + HALO, chunk, main, rest)

    each_chunk(first.shape[1] - 2, body)


def first_kernel(dense, gain_pad, weight, weight_hbm, first, wire, later_weight, hidden, sem):
    copy = pltpu.make_async_copy(weight_hbm.at[pl.ds(1, later_weight.shape[0])], later_weight, sem)
    copy.start()
    hidden[:, 1] = jnp.zeros_like(hidden[:, 1])
    for frame in range(STAGED, dense.shape[0]):
        dense_in(dense, first, frame, gain_pad, weight.shape[-1])
    hidden_out(first, HALO, weight.at[0], 0, hidden, gain_pad, 1, None, wire, OLD_FIRST, WHOLE)
    copy.wait()


def convolve_frames(source, base, weight, layer, hidden, taps, splits, finish):
    cols = source.shape[1] - 2
    part = cols // splits
    for first_col in range(0, cols, part):
        for i in range(HALO):
            slot = 2 * (layer % 2) + i
            convolve(source, base + i, weight, hidden, slot, first_col, part, taps)
            for chunk in range(first_col // STEP, (first_col + part) // STEP):
                finish(i, chunk, *hidden_chunk(hidden, slot, chunk))


def hidden_out(source, base, weight, layer, hidden, gain_pad, gain_index, target, wire, taps, splits):
    channels = weight.shape[-1]

    def finish(i, chunk, main, rest):
        main, rest = activate(main, rest, *load_gain(gain_pad, gain_index), channels)
        if wire is None:
            store_pieces(target, base + HALO + i, chunk, main, rest)
        else:
            pack_wire(wire, i, chunk, main, rest)

    convolve_frames(source, base, weight, layer, hidden, taps, splits, finish)


def residual_out(source, base, weight, layer, hidden, taps, splits, finish):
    convolve_frames(source, base, weight, layer, hidden, taps, splits, finish)


def rounded(value):
    return value.astype(jnp.bfloat16).astype(jnp.float32)


def state_put(state, i, chunk, main, rest):
    state[i, 0, pl.ds(STEP * chunk, STEP)] = main.astype(state.dtype)
    state[i, 1, pl.ds(STEP * chunk, STEP)] = rest.astype(state.dtype)


def state_get(state, i, chunk):
    return (
        state[i, 0, pl.ds(STEP * chunk, STEP)].astype(jnp.float32),
        state[i, 1, pl.ds(STEP * chunk, STEP)].astype(jnp.float32),
    )


def wire_in(read, target, base):
    cols = target.shape[1] - 2
    for frame in range(HALO):
        each_chunk(cols, lambda chunk: store_pieces(target, base + frame, chunk, *unpack_wire(read, cols, frame, chunk)))


def halo_in(read, target, keep):
    wire_in(lambda index: read(index) * keep, target, 0)


def own_in(read, target):
    wire_in(read, target, 2 * HALO)


def second_kernel(
    facts, halo, dense, gain_pad, own, weight, later_weight, first, second, state, wire, hidden
):
    cols = first.shape[1] - 2
    channels = later_weight.shape[-1]
    keep = facts[0][None, None, :]
    clear_borders(second)
    own_in(plain(own), second)
    hidden[:, 1] = jnp.zeros_like(hidden[:, 1])

    def enter(frame):
        def body(chunk):
            main, rest = unpack_dense(halo[dense_chunk(frame, chunk)])
            main, rest = activate(main, rest, *load_gain(gain_pad, 0), channels)
            store_pieces(first, frame, chunk, main * keep, rest * keep)

        each_chunk(cols, body)

    each_frame(HALO, enter)
    hidden_out(first, 0, weight.at[0], 0, hidden, gain_pad, 1, second, None, NEW_FIRST, WHOLE)

    def finish(i, chunk, main, rest):
        main_in, rest_in = unpack_dense(dense[dense_chunk(HALO + i, chunk)])
        main, rest = rounded(main + main_in), rounded(rest + rest_in)
        state_put(state, i, chunk, main, rest)
        main, rest = activate(main, rest, *load_gain(gain_pad, 2), channels)
        pack_wire(wire, i, chunk, main, rest)

    residual_out(second, HALO, later_weight.at[0], 1, hidden, NEW_FIRST, LAST_SPLIT, finish)


def third_kernel(
    facts, halo, dense, gain_pad, own, later_weight, second, third, state, wire, hidden
):
    channels = later_weight.shape[-1]
    keep = facts[0][None, None, :]
    clear_borders(third)
    own_in(plain(own), third)
    hidden[:, 1] = jnp.zeros_like(hidden[:, 1])
    halo_in(plain(halo), second, keep)

    def finish(i, chunk, main, rest):
        main_in, rest_in = unpack_dense(dense[dense_chunk(i, chunk)])
        main, rest = rounded(main + main_in), rounded(rest + rest_in)
        state_put(state, i, chunk, main, rest)
        main, rest = activate(main, rest, *load_gain(gain_pad, 2), channels)
        store_pieces(third, HALO + i, chunk, main, rest)

    residual_out(second, 0, later_weight.at[0], 1, hidden, NEW_FIRST, WHOLE, finish)
    hidden_out(third, HALO, later_weight.at[1], 2, hidden, gain_pad, 3, None, wire, NEW_FIRST, LAST_SPLIT)


def fourth_kernel(
    facts, swapped, crossed, gain_pad, own_odd, own_even, later_weight, third_in, state, third, fourth, out, hidden
):
    keep = facts[0][None, None, :]
    clear_borders(fourth)
    own_in(by_place(own_even, own_odd), fourth)
    hidden[:, 1] = jnp.zeros_like(hidden[:, 1])
    halo_in(by_place(crossed, swapped), third, keep)
    hidden_out(third, 0, later_weight.at[1], 2, hidden, gain_pad, 3, fourth, None, NEW_FIRST, WHOLE)

    def finish(i, chunk, main, rest):
        main_in, rest_in = state_get(state, i, chunk)
        live = facts[1 + HALO + i][None, None, :]
        pack_dense(out, i, chunk, (main + main_in) * live, (rest + rest_in) * live)

    residual_out(fourth, HALO, later_weight.at[2], 3, hidden, NEW_FIRST, LAST_SPLIT, finish)


def fifth_kernel(
    facts, swapped, crossed, later_weight, fourth_in, state, later, fourth, out, hidden, stage, sems
):
    keep = facts[0][None, None, :]
    copies = [pltpu.make_async_copy(later, out.at[pl.ds(HALO, HALO)], sems.at[0])]
    copies[0].start()
    hidden[:, 1] = jnp.zeros_like(hidden[:, 1])
    halo_in(by_place(crossed, swapped), fourth, keep)
    width = stage.shape[2] // END_SPLIT
    chunks = (fourth.shape[1] - 2) // (STEP * END_SPLIT)

    def finish(i, chunk, main, rest):
        main_in, rest_in = state_get(state, i, chunk)
        live = facts[1 + i][None, None, :]
        pack_dense(stage, i, chunk, (main + main_in) * live, (rest + rest_in) * live)
        if (chunk + 1) % chunks == 0:
            part = chunk // chunks
            lanes = pl.ds(part * width, width)
            sem = sems.at[1 + HALO * part + i]
            copies.append(pltpu.make_async_copy(stage.at[i, :, lanes], out.at[i, :, lanes], sem))
            copies[-1].start()

    residual_out(fourth, 0, later_weight.at[2], 3, hidden, NEW_FIRST, END_SPLIT, finish)
    for copy in copies:
        copy.wait()


def local(features, gains, conv_weights, video_frames, video_start):
    frames, rows, merged = features.shape
    channels = gains.shape[1]
    cols = merged // channels
    layers = conv_weights.shape[0]
    weight = conv_weights.reshape(layers, 27, channels, channels)
    bf16, f32 = jnp.bfloat16, jnp.float32
    pieces = jax.ShapeDtypeStruct((frames + HALO, cols + 2, rows, 5 * LANES), bf16)
    wire = jax.ShapeDtypeStruct((HALO, cols * 3 // 2, rows, LANES), bf16)
    state = jax.ShapeDtypeStruct((HALO, 2, cols, rows, LANES), bf16)
    hidden = VMEM((2 * HALO, 2, cols, rows, LANES), f32)
    vmem = pl.BlockSpec(memory_space=VMEM)
    hbm = pl.BlockSpec(memory_space=pltpu.HBM)

    def call(body, ins, outs, scratch, convs, aliases=None, out_specs=None):
        return pl.pallas_call(
            body,
            out_shape=outs,
            in_specs=ins,
            out_specs=out_specs or tuple(vmem for _ in outs),
            scratch_shapes=scratch,
            input_output_aliases=aliases or {},
            compiler_params=pltpu.CompilerParams(vmem_limit_bytes=12 << 20),
            cost_estimate=pl.CostEstimate(
                flops=convs * 2 * 27 * channels * channels * rows * cols * 2,
                bytes_accessed=4 << 20,
                transcendentals=0,
            ),
        )

    def weights(count):
        return jax.ShapeDtypeStruct((count, 27, channels, channels), bf16)

    dense = jax.ShapeDtypeStruct(features.shape, bf16)
    dense_half = jax.ShapeDtypeStruct((HALO, rows, merged), bf16)
    dma = pltpu.SemaphoreType.DMA
    facts = jax.ShapeDtypeStruct((8, LANES), f32)
    gain_rows = jax.ShapeDtypeStruct((layers, 2, LANES), f32)
    in_hbm = [
        pltpu.with_memory_space_constraint(a, pltpu.HBM)
        for a in (features, gains, weight, video_start, video_frames)
    ]
    weight_hbm = in_hbm[2]
    count = lax.axis_size("tm")
    swap = [(i, i ^ 1) for i in range(count)]
    cross = [(i, i + 1) for i in range(1, count - 1, 2)]

    def half(body, odd, ins, specs, carried, outs, scratch, convs):
        kernel = at_place(body, odd, len(ins), len(carried))
        aliases = {len(ins) + n: index for n, index in enumerate(carried)}
        arrays = (*ins, *carried.values())
        return call(kernel, specs + [vmem] * len(carried), outs, scratch, convs, aliases)(*arrays)

    def exchange(sent, even_step, swapped_of, next_step):
        crossed = lax.ppermute(sent, "tm", cross)
        even = even_step()
        swapped = lax.ppermute(even[swapped_of], "tm", swap)
        after = next_step(even, swapped)
        return crossed, swapped, even, after

    def stage(odd, carried):
        outs = (pieces, dense_half, dense, weights(1), gain_rows, facts)
        small = pltpu.SMEM(video_start.shape, jnp.int32)
        scratch = [VMEM(gains.shape, f32), small, small, dma((6,))]
        return half(stage_kernel, odd, in_hbm, [hbm] * 5, carried, outs, scratch, 0)

    def step1(odd, staged, carried):
        _, _, block, weight0, gain_rows, _ = staged
        return half(
            first_kernel,
            odd,
            (block, gain_rows, weight0, weight_hbm),
            [vmem, vmem, vmem, hbm],
            carried,
            (pieces, wire, weights(layers - 1)),
            [hidden, dma],
            1,
        )

    def step2(odd, known, halo, block, own, weight0, later_weight, carried):
        return half(
            second_kernel,
            odd,
            (known[1], halo, block, known[0], own, weight0, later_weight),
            [vmem] * 7,
            carried,
            (pieces, pieces, state, wire),
            [hidden],
            2,
        )

    def step3(odd, known, halo, block, own, later_weight, carried):
        return half(
            third_kernel,
            odd,
            (known[1], halo, block, known[0], own, later_weight),
            [vmem] * 6,
            carried,
            (pieces, pieces, state, wire),
            [hidden],
            2,
        )

    odd0 = stage(True, {})
    crossed0, swapped0, staged, odd1 = exchange(
        odd0[1],
        lambda: stage(False, {n: odd0[n] for n in (0, 2, 3, 4, 5)}),
        1,
        lambda staged, _: step1(True, staged, {0: staged[0]}),
    )
    block, weight0, known = staged[2], staged[3], staged[4:]
    crossed1, swapped1, even1, odd2 = exchange(
        odd1[1],
        lambda: step1(False, staged, {0: odd1[0], 2: odd1[2]}),
        1,
        lambda even, _: step2(True, known, swapped0, block, odd1[1], weight0, even[2], {0: even[0]}),
    )
    later_weight = even1[2]
    crossed2, swapped2, even2, odd3 = exchange(
        odd2[3],
        lambda: step2(
            False, known, crossed0, block, even1[1], weight0, later_weight, {0: odd2[0], 1: odd2[1], 2: odd2[2]}
        ),
        3,
        lambda even, _: step3(True, known, swapped1, block, odd2[3], later_weight, {0: even[1]}),
    )
    state_late = even2[2]

    def last_steps(even, swapped):
        third = even[1]
        return call(
            fourth_kernel, [vmem] * 9, (pieces, pieces, dense_half), [hidden], 2, {7: 0}
        )(known[1], swapped2, crossed2, known[0], odd3[3], even[3], later_weight, third, state_late)

    crossed3, swapped3, even3, (_, fourth, later) = exchange(
        odd3[3],
        lambda: step3(False, known, crossed1, block, even2[3], later_weight, {0: odd3[0], 1: odd3[1], 2: odd3[2]}),
        3,
        last_steps,
    )
    _, out = call(
        fifth_kernel,
        [vmem] * 7,
        (pieces, dense),
        [hidden, VMEM(dense_half.shape, bf16), dma((1 + HALO * END_SPLIT,))],
        1,
        {4: 0},
        (vmem, hbm),
    )(known[1], swapped3, crossed3, later_weight, fourth, even3[2], later)
    return out


def solution(mesh):
    in_specs = (P(("grp", "tm"), None, None), P(), P(), P("grp"), P("grp"))
    out_specs = P(("grp", "tm"), None, None)
    return jax.shard_map(local, mesh=mesh, in_specs=in_specs, out_specs=out_specs, check_vma=False)
```

```python
import jax
import jax.numpy as jnp
from jax import lax
from jax.experimental import pallas as pl
from jax.experimental.pallas import tpu as pltpu
from jax.sharding import PartitionSpec as P


LANES = 128
HALO = 2
STEP = 4
STAGED = 0
OLD_FIRST = (0, 1, 2)
NEW_FIRST = (2, 1, 0)
WHOLE = 1
LAST_SPLIT = 2
END_SPLIT = 2
VMEM = pltpu.VMEM


def is_odd():
    return lax.rem(lax.axis_index("tm"), 2) == 1


def plain(ref):
    return lambda index: ref[index].astype(jnp.float32)


def by_place(even_ref, odd_ref):
    odd = is_odd()
    return lambda index: jnp.where(odd, odd_ref[index].astype(jnp.float32), even_ref[index].astype(jnp.float32))


def at_place(body, odd, inputs, carried):
    def kernel(*refs):
        @pl.when(is_odd() == odd)
        def _():
            body(*refs[:inputs], *refs[inputs + carried :])

    return kernel


def low_half(shape):
    return lax.broadcasted_iota(jnp.int32, shape, len(shape) - 1) < LANES // 2


def swap_half(value):
    return pltpu.roll(value, LANES // 2, axis=value.ndim - 1)


def activate(main, rest, gain_main, gain_rest, channels):
    total = jnp.sum(main * main + rest * rest, axis=-1, keepdims=True)
    inverse = lax.rsqrt(total * (1.0 / channels) + 1e-06)

    def silu(value, gain):
        scaled = value * inverse * gain
        half = 0.5 * scaled
        return half * jnp.tanh(half) + half

    return silu(main, gain_main), silu(rest, gain_rest)


def load_gain(gain_pad, index):
    return gain_pad[index, 0][None, None, :], gain_pad[index, 1][None, None, :]


def fill_gain(gains, gain_pad):
    count, channels = gains.shape
    gain_pad[...] = jnp.zeros_like(gain_pad)
    for k in range(count):
        gain_pad[k, 0:1, :] = gains[k : k + 1, 0:LANES]
        gain_pad[k, 1:2, 0 : channels - LANES] = gains[k : k + 1, LANES:channels]


def dense_chunk(frame, chunk):
    width = STEP * 192
    return (frame, slice(None), slice(chunk * width, (chunk + 1) * width))


def unpack_dense(block):
    rows, width = block.shape
    block = block.astype(jnp.float32)
    tile = [block[:, LANES * i : LANES * (i + 1)] for i in range(width // LANES)]
    low = low_half((rows, LANES))
    main, rest = [], []
    for i in range(0, len(tile), 3):
        rolled_b, rolled_c = swap_half(tile[i + 1]), swap_half(tile[i + 2])
        main += [tile[i], jnp.where(low, rolled_b, rolled_c)]
        rest += [jnp.where(low, tile[i + 1], 0.0), jnp.where(low, rolled_c, 0.0)]
    return jnp.stack(main), jnp.stack(rest)


def pack_dense(target, frame, chunk, main, rest):
    rows = target.shape[1]
    width = STEP * 192
    low = low_half((rows, LANES))
    tile = []
    for i in range(0, STEP, 2):
        rolled = swap_half(main[i + 1])
        tile += [main[i], jnp.where(low, rest[i], rolled), jnp.where(low, rolled, swap_half(rest[i + 1]))]
    block = jnp.concatenate(tile, axis=-1).astype(target.dtype)
    target[frame, :, chunk * width : (chunk + 1) * width] = block


def unpack_wire(read, cols, frame, chunk):
    main = read((frame, pl.ds(STEP * chunk, STEP)))
    pair = read((frame, pl.ds(cols + STEP // 2 * chunk, STEP // 2)))
    low = low_half(pair.shape)
    rest = jnp.stack([jnp.where(low, pair, 0.0), jnp.where(low, swap_half(pair), 0.0)], axis=1)
    return main, rest.reshape(main.shape)


def pack_wire(target, frame, chunk, main, rest):
    cols = target.shape[1] * 2 // 3
    target[frame, pl.ds(STEP * chunk, STEP)] = main.astype(target.dtype)
    pair = rest.reshape((STEP // 2, 2) + rest.shape[1:])
    target[frame, pl.ds(cols + STEP // 2 * chunk, STEP // 2)] = (pair[:, 0] + swap_half(pair[:, 1])).astype(target.dtype)


def clear_borders(buf):
    frames, slots, rows, lanes = buf.shape
    for frame in range(frames):
        for slot in (0, slots - 2, slots - 1):
            buf[frame, slot] = jnp.zeros((rows, lanes), buf.dtype)


def store_pieces(buf, frame, chunk, main, rest):
    rows = main.shape[1]
    row = lax.broadcasted_iota(jnp.int32, main.shape, 1)

    def above(value):
        return jnp.where(row == 0, 0.0, pltpu.roll(value, 1, axis=1))

    def below(value):
        return jnp.where(row == rows - 1, 0.0, pltpu.roll(value, rows - 1, axis=1))

    def put(first_slot, lane, value):
        buf[frame, pl.ds(first_slot, STEP), :, lane : lane + value.shape[-1]] = value.astype(buf.dtype)

    slot = STEP * chunk + 1
    put(slot, 0, above(main))
    put(slot, LANES, main)
    put(slot, 2 * LANES, below(main))
    put(slot, 3 * LANES, above(rest) + swap_half(rest))
    lower = below(rest)
    put(slot, 4 * LANES, lower[..., : LANES // 2])
    put(slot - 1, 4 * LANES + LANES // 2, lower[..., : LANES // 2])


def convolve(buf, frame, weight, hidden, slot, first_col, cols, taps):
    rows = buf.shape[2]
    channels = weight.shape[-1]
    span = channels - LANES

    def piece(tap, col, lane):
        return buf[frame + tap, first_col + col : first_col + col + cols, :, lane : lane + LANES].reshape(cols * rows, LANES)

    def taken(tap, row, col, rest):
        index = (tap * 3 + row) * 3 + col
        return weight[index, LANES:channels, :] if rest else weight[index, 0:LANES, :]

    lhs, rhs = [], []
    for tap in taps:
        for col in range(3):
            for row in range(3):
                lhs.append(piece(tap, col, LANES * row))
                rhs.append(taken(tap, row, col, False))
            lhs.append(piece(tap, col, 3 * LANES))
            rhs += [taken(tap, 0, col, True), taken(tap, 1, col, True)]
        lhs.append(piece(tap, 0, 4 * LANES))
        rhs += [taken(tap, 2, 0, True), taken(tap, 2, 1, True)]
        lhs.append(piece(tap, 2, 4 * LANES))
        rhs += [taken(tap, 2, 2, True), jnp.zeros((span, channels), weight.dtype)]
    total = jnp.dot(jnp.concatenate(lhs, axis=1), jnp.concatenate(rhs, axis=0), preferred_element_type=jnp.float32)
    hidden[slot, 0, first_col : first_col + cols] = total[:, :LANES].reshape(cols, rows, LANES)
    hidden[slot, 1, first_col : first_col + cols, :, 0:span] = total[:, LANES:].reshape(cols, rows, span)


def each_chunk(cols, body):
    for chunk in range(cols // STEP):
        body(chunk)


def each_frame(count, body):
    for index in range(count):
        body(index)


def hidden_chunk(hidden, slot, chunk):
    return hidden[slot, 0, pl.ds(STEP * chunk, STEP)], hidden[slot, 1, pl.ds(STEP * chunk, STEP)]


def own_span(starts, frames):
    span = lax.axis_index("tm")
    own_start, own_frames = starts[0], frames[0]
    for v in range(1, starts.shape[0]):
        here = starts[v] <= span
        own_start = jnp.where(here, starts[v], own_start)
        own_frames = jnp.where(here, frames[v], own_frames)
    return span, own_start, own_frames


def stage_kernel(
    dense_hbm, gains_hbm, weight_hbm, starts_hbm, frames_hbm, first, wire, dense, weight, gain_pad, facts, gains, starts, frames, sems
):
    copies = [
        pltpu.make_async_copy(dense_hbm, dense, sems.at[0]),
        pltpu.make_async_copy(gains_hbm, gains, sems.at[1]),
        pltpu.make_async_copy(dense_hbm.at[pl.ds(HALO, HALO)], wire, sems.at[2]),
        pltpu.make_async_copy(starts_hbm, starts, sems.at[3]),
        pltpu.make_async_copy(frames_hbm, frames, sems.at[4]),
        pltpu.make_async_copy(weight_hbm.at[pl.ds(0, 1)], weight, sems.at[5]),
    ]
    for copy in copies:
        copy.start()
    clear_borders(first)
    for copy in copies[:5]:
        copy.wait()
    fill_gain(gains, gain_pad)
    span, own_start, own_frames = own_span(starts, frames)
    factors = [jnp.where(span - 1 >= own_start, 1.0, 0.0)]
    for frame in range(2 * HALO):
        factors.append(jnp.where((span - own_start) * (2 * HALO) + frame < own_frames, 1.0, 0.0))
    for row, factor in enumerate(factors):
        facts[row] = jnp.full((LANES,), factor, facts.dtype)
    for frame in range(STAGED):
        dense_in(dense, first, frame, gain_pad, gains.shape[1])
    copies[5].wait()


def dense_in(dense, first, frame, gain_pad, channels):
    def body(chunk):
        main, rest = unpack_dense(dense[dense_chunk(frame, chunk)])
        main, rest = activate(main, rest, *load_gain(gain_pad, 0), channels)
        store_pieces(first, frame + HALO, chunk, main, rest)

    each_chunk(first.shape[1] - 2, body)


def first_kernel(dense, gain_pad, weight, weight_hbm, first, wire, later_weight, hidden, sem):
    copy = pltpu.make_async_copy(weight_hbm.at[pl.ds(1, later_weight.shape[0])], later_weight, sem)
    copy.start()
    hidden[:, 1] = jnp.zeros_like(hidden[:, 1])
    for frame in range(STAGED, dense.shape[0]):
        dense_in(dense, first, frame, gain_pad, weight.shape[-1])
    hidden_out(first, HALO, weight.at[0], 0, hidden, gain_pad, 1, None, wire, OLD_FIRST, WHOLE)
    copy.wait()


def convolve_frames(source, base, weight, layer, hidden, taps, splits, finish):
    cols = source.shape[1] - 2
    part = cols // splits
    for first_col in range(0, cols, part):
        for i in range(HALO):
            slot = 2 * (layer % 2) + i
            convolve(source, base + i, weight, hidden, slot, first_col, part, taps)
            for chunk in range(first_col // STEP, (first_col + part) // STEP):
                finish(i, chunk, *hidden_chunk(hidden, slot, chunk))


def hidden_out(source, base, weight, layer, hidden, gain_pad, gain_index, target, wire, taps, splits):
    channels = weight.shape[-1]

    def finish(i, chunk, main, rest):
        main, rest = activate(main, rest, *load_gain(gain_pad, gain_index), channels)
        if wire is None:
            store_pieces(target, base + HALO + i, chunk, main, rest)
        else:
            pack_wire(wire, i, chunk, main, rest)

    convolve_frames(source, base, weight, layer, hidden, taps, splits, finish)


def residual_out(source, base, weight, layer, hidden, taps, splits, finish):
    convolve_frames(source, base, weight, layer, hidden, taps, splits, finish)


def rounded(value):
    return value.astype(jnp.bfloat16).astype(jnp.float32)


def state_put(state, i, chunk, main, rest):
    state[i, 0, pl.ds(STEP * chunk, STEP)] = main.astype(state.dtype)
    state[i, 1, pl.ds(STEP * chunk, STEP)] = rest.astype(state.dtype)


def state_get(state, i, chunk):
    return (
        state[i, 0, pl.ds(STEP * chunk, STEP)].astype(jnp.float32),
        state[i, 1, pl.ds(STEP * chunk, STEP)].astype(jnp.float32),
    )


def wire_in(read, target, base):
    cols = target.shape[1] - 2
    for frame in range(HALO):
        each_chunk(cols, lambda chunk: store_pieces(target, base + frame, chunk, *unpack_wire(read, cols, frame, chunk)))


def halo_in(read, target, keep):
    wire_in(lambda index: read(index) * keep, target, 0)


def own_in(read, target):
    wire_in(read, target, 2 * HALO)


def second_kernel(
    facts, halo, dense, gain_pad, own, weight, later_weight, weight_hbm, first, second, state, wire, last_weight, hidden, sem
):
    cols = first.shape[1] - 2
    channels = later_weight.shape[-1]
    keep = facts[0][None, None, :]
    copy = pltpu.make_async_copy(weight_hbm.at[pl.ds(2, last_weight.shape[0])], last_weight, sem)
    copy.start()
    clear_borders(second)
    own_in(plain(own), second)
    hidden[:, 1] = jnp.zeros_like(hidden[:, 1])

    def enter(frame):
        def body(chunk):
            main, rest = unpack_dense(halo[dense_chunk(frame, chunk)])
            main, rest = activate(main, rest, *load_gain(gain_pad, 0), channels)
            store_pieces(first, frame, chunk, main * keep, rest * keep)

        each_chunk(cols, body)

    each_frame(HALO, enter)
    hidden_out(first, 0, weight.at[0], 0, hidden, gain_pad, 1, second, None, NEW_FIRST, WHOLE)

    def finish(i, chunk, main, rest):
        main_in, rest_in = unpack_dense(dense[dense_chunk(HALO + i, chunk)])
        main, rest = rounded(main + main_in), rounded(rest + rest_in)
        state_put(state, i, chunk, main, rest)
        main, rest = activate(main, rest, *load_gain(gain_pad, 2), channels)
        pack_wire(wire, i, chunk, main, rest)

    residual_out(second, HALO, later_weight.at[0], 1, hidden, NEW_FIRST, LAST_SPLIT, finish)
    copy.wait()


def third_kernel(
    facts, halo, dense, gain_pad, own, later_weight, last_weight, second, third, state, wire, hidden
):
    channels = later_weight.shape[-1]
    keep = facts[0][None, None, :]
    clear_borders(third)
    own_in(plain(own), third)
    hidden[:, 1] = jnp.zeros_like(hidden[:, 1])
    halo_in(plain(halo), second, keep)

    def finish(i, chunk, main, rest):
        main_in, rest_in = unpack_dense(dense[dense_chunk(i, chunk)])
        main, rest = rounded(main + main_in), rounded(rest + rest_in)
        state_put(state, i, chunk, main, rest)
        main, rest = activate(main, rest, *load_gain(gain_pad, 2), channels)
        store_pieces(third, HALO + i, chunk, main, rest)

    residual_out(second, 0, later_weight.at[0], 1, hidden, NEW_FIRST, WHOLE, finish)
    hidden_out(third, HALO, last_weight.at[0], 2, hidden, gain_pad, 3, None, wire, NEW_FIRST, LAST_SPLIT)


def fourth_kernel(
    facts, swapped, crossed, gain_pad, own_odd, own_even, last_weight, third_in, state, third, fourth, out, hidden
):
    keep = facts[0][None, None, :]
    clear_borders(fourth)
    own_in(by_place(own_even, own_odd), fourth)
    hidden[:, 1] = jnp.zeros_like(hidden[:, 1])
    halo_in(by_place(crossed, swapped), third, keep)
    hidden_out(third, 0, last_weight.at[0], 2, hidden, gain_pad, 3, fourth, None, NEW_FIRST, WHOLE)

    def finish(i, chunk, main, rest):
        main_in, rest_in = state_get(state, i, chunk)
        live = facts[1 + HALO + i][None, None, :]
        pack_dense(out, i, chunk, (main + main_in) * live, (rest + rest_in) * live)

    residual_out(fourth, HALO, last_weight.at[1], 3, hidden, NEW_FIRST, LAST_SPLIT, finish)


def fifth_kernel(
    facts, swapped, crossed, last_weight, fourth_in, state, later, fourth, out, hidden, stage, sems
):
    keep = facts[0][None, None, :]
    copies = [pltpu.make_async_copy(later, out.at[pl.ds(HALO, HALO)], sems.at[0])]
    copies[0].start()
    hidden[:, 1] = jnp.zeros_like(hidden[:, 1])
    halo_in(by_place(crossed, swapped), fourth, keep)
    width = stage.shape[2] // END_SPLIT
    chunks = (fourth.shape[1] - 2) // (STEP * END_SPLIT)

    def finish(i, chunk, main, rest):
        main_in, rest_in = state_get(state, i, chunk)
        live = facts[1 + i][None, None, :]
        pack_dense(stage, i, chunk, (main + main_in) * live, (rest + rest_in) * live)
        if (chunk + 1) % chunks == 0:
            part = chunk // chunks
            lanes = pl.ds(part * width, width)
            sem = sems.at[1 + HALO * part + i]
            copies.append(pltpu.make_async_copy(stage.at[i, :, lanes], out.at[i, :, lanes], sem))
            copies[-1].start()

    residual_out(fourth, 0, last_weight.at[1], 3, hidden, NEW_FIRST, END_SPLIT, finish)
    for copy in copies:
        copy.wait()


def local(features, gains, conv_weights, video_frames, video_start):
    frames, rows, merged = features.shape
    channels = gains.shape[1]
    cols = merged // channels
    layers = conv_weights.shape[0]
    weight = conv_weights.reshape(layers, 27, channels, channels)
    bf16, f32 = jnp.bfloat16, jnp.float32
    pieces = jax.ShapeDtypeStruct((frames + HALO, cols + 2, rows, 5 * LANES), bf16)
    wire = jax.ShapeDtypeStruct((HALO, cols * 3 // 2, rows, LANES), bf16)
    state = jax.ShapeDtypeStruct((HALO, 2, cols, rows, LANES), bf16)
    hidden = VMEM((2 * HALO, 2, cols, rows, LANES), f32)
    vmem = pl.BlockSpec(memory_space=VMEM)
    hbm = pl.BlockSpec(memory_space=pltpu.HBM)

    def call(body, ins, outs, scratch, convs, aliases=None, out_specs=None):
        return pl.pallas_call(
            body,
            out_shape=outs,
            in_specs=ins,
            out_specs=out_specs or tuple(vmem for _ in outs),
            scratch_shapes=scratch,
            input_output_aliases=aliases or {},
            compiler_params=pltpu.CompilerParams(vmem_limit_bytes=12 << 20),
            cost_estimate=pl.CostEstimate(
                flops=convs * 2 * 27 * channels * channels * rows * cols * 2,
                bytes_accessed=4 << 20,
                transcendentals=0,
            ),
        )

    def weights(count):
        return jax.ShapeDtypeStruct((count, 27, channels, channels), bf16)

    dense = jax.ShapeDtypeStruct(features.shape, bf16)
    dense_half = jax.ShapeDtypeStruct((HALO, rows, merged), bf16)
    dma = pltpu.SemaphoreType.DMA
    facts = jax.ShapeDtypeStruct((8, LANES), f32)
    gain_rows = jax.ShapeDtypeStruct((layers, 2, LANES), f32)
    in_hbm = [
        pltpu.with_memory_space_constraint(a, pltpu.HBM)
        for a in (features, gains, weight, video_start, video_frames)
    ]
    weight_hbm = in_hbm[2]
    count = lax.axis_size("tm")
    swap = [(i, i ^ 1) for i in range(count)]
    cross = [(i, i + 1) for i in range(1, count - 1, 2)]

    def half(body, odd, ins, specs, carried, outs, scratch, convs):
        kernel = at_place(body, odd, len(ins), len(carried))
        aliases = {len(ins) + n: index for n, index in enumerate(carried)}
        arrays = (*ins, *carried.values())
        return call(kernel, specs + [vmem] * len(carried), outs, scratch, convs, aliases)(*arrays)

    def exchange(sent, even_step, swapped_of, next_step):
        crossed = lax.ppermute(sent, "tm", cross)
        even = even_step()
        swapped = lax.ppermute(even[swapped_of], "tm", swap)
        after = next_step(even, swapped)
        return crossed, swapped, even, after

    def stage(odd, carried):
        outs = (pieces, dense_half, dense, weights(1), gain_rows, facts)
        small = pltpu.SMEM(video_start.shape, jnp.int32)
        scratch = [VMEM(gains.shape, f32), small, small, dma((6,))]
        return half(stage_kernel, odd, in_hbm, [hbm] * 5, carried, outs, scratch, 0)

    def step1(odd, staged, carried):
        _, _, block, weight0, gain_rows, _ = staged
        return half(
            first_kernel,
            odd,
            (block, gain_rows, weight0, weight_hbm),
            [vmem, vmem, vmem, hbm],
            carried,
            (pieces, wire, weights(1)),
            [hidden, dma],
            1,
        )

    def step2(odd, known, halo, block, own, weight0, later_weight, carried):
        return half(
            second_kernel,
            odd,
            (known[1], halo, block, known[0], own, weight0, later_weight, weight_hbm),
            [vmem] * 7 + [hbm],
            carried,
            (pieces, pieces, state, wire, weights(layers - 2)),
            [hidden, dma],
            2,
        )

    def step3(odd, known, halo, block, own, later_weight, last_weight, carried):
        return half(
            third_kernel,
            odd,
            (known[1], halo, block, known[0], own, later_weight, last_weight),
            [vmem] * 7,
            carried,
            (pieces, pieces, state, wire),
            [hidden],
            2,
        )

    odd0 = stage(True, {})
    crossed0, swapped0, staged, odd1 = exchange(
        odd0[1],
        lambda: stage(False, {n: odd0[n] for n in (0, 2, 3, 4, 5)}),
        1,
        lambda staged, _: step1(True, staged, {0: staged[0]}),
    )
    block, weight0, known = staged[2], staged[3], staged[4:]
    crossed1, swapped1, even1, odd2 = exchange(
        odd1[1],
        lambda: step1(False, staged, {0: odd1[0], 2: odd1[2]}),
        1,
        lambda even, _: step2(True, known, swapped0, block, odd1[1], weight0, even[2], {0: even[0]}),
    )
    later_weight = even1[2]
    crossed2, swapped2, even2, odd3 = exchange(
        odd2[3],
        lambda: step2(
            False, known, crossed0, block, even1[1], weight0, later_weight, {n: odd2[n] for n in (0, 1, 2, 4)}
        ),
        3,
        lambda even, _: step3(True, known, swapped1, block, odd2[3], later_weight, even[4], {0: even[1]}),
    )
    state_late, last_weight = even2[2], even2[4]

    def last_steps(even, swapped):
        third = even[1]
        return call(
            fourth_kernel, [vmem] * 9, (pieces, pieces, dense_half), [hidden], 2, {7: 0}
        )(known[1], swapped2, crossed2, known[0], odd3[3], even[3], last_weight, third, state_late)

    crossed3, swapped3, even3, (_, fourth, later) = exchange(
        odd3[3],
        lambda: step3(
            False, known, crossed1, block, even2[3], later_weight, last_weight, {0: odd3[0], 1: odd3[1], 2: odd3[2]}
        ),
        3,
        last_steps,
    )
    _, out = call(
        fifth_kernel,
        [vmem] * 7,
        (pieces, dense),
        [hidden, VMEM(dense_half.shape, bf16), dma((1 + HALO * END_SPLIT,))],
        1,
        {4: 0},
        (vmem, hbm),
    )(known[1], swapped3, crossed3, last_weight, fourth, even3[2], later)
    return out


def solution(mesh):
    in_specs = (P(("grp", "tm"), None, None), P(), P(), P("grp"), P("grp"))
    out_specs = P(("grp", "tm"), None, None)
    return jax.shard_map(local, mesh=mesh, in_specs=in_specs, out_specs=out_specs, check_vma=False)
```
